32 devices in a mesh: rep: 2 (over y), seq: 4 (over z), head: 4 (over x, core).
Axes of the slice: x: 2, y: 2, z: 4, core: 2. Of those that a mesh axis runs over, the one named last changes fastest.
Arguments:
- queries: bfloat16 [5120, 4096], P(('rep', 'seq'), 'head'), parts along dimension 0, may hold values from -5 to 5
- keys: bfloat16 [5120, 4096], P(('rep', 'seq'), 'head'), parts along dimension 0, may hold values from -5 to 5
- values: bfloat16 [5120, 4096], P(('rep', 'seq'), 'head'), parts along dimension 0, may hold values from -6 to 6
- d_out: bfloat16 [5120, 4096], P(('rep', 'seq'), 'head'), parts along dimension 0, may hold values from -6 to 6
- shift: int32 [2], P('rep'), parts along dimension 0, may hold values from 160 to 480
- head_order: int32 [32], replicated, may hold values from 0 to 31, each once
Outputs:
- d_queries: bfloat16 [5120, 4096], P(('rep', 'seq'), 'head'), parts along dimension 0
- d_keys: bfloat16 [5120, 4096], P(('rep', 'seq'), 'head'), parts along dimension 0
- d_values: bfloat16 [5120, 4096], P(('rep', 'seq'), 'head'), parts along dimension 0
The draws below stay inside these ranges and needn't reach their ends.
There are 2 independent parts, one for each index of `rep`. The reference program is written for one: setup_inputs(seed, part) draws one part's arguments, and reference() takes and returns one part's arrays. A program takes and returns all parts, laid end to end along the dimension named above; an argument that names none is the same for every part. Nothing has to cross between parts.
Inputs may be any that keep to these rules, and one draw needn't show every extreme that they name: head_order is a permutation of the 32 heads.
All inputs are finite; a program needn't handle non-finite values.
Results may differ from the reference program's by a relative error of at most 0.01.
Values may be sent and summed in bfloat16 or wider, within the bound.
No kernel may reach another device: no remote copies, remote signals or barrier semaphores. Data moves between devices by JAX's collectives and lax.ppermute only.
A program may use at most 64 MiB of HBM per device.

```python
import jax
import jax.numpy as jnp
from jax import lax

TOK_DEV = 640
HEADS = 32
HDIM = 128
TOKENS = 2560


def base_field(key):
    width = HEADS * HDIM
    return jnp.clip(jax.random.normal(jax.random.fold_in(key, 3), (TOKENS, width), jnp.float32), -4.0, 4.0)


def draw_queries(key, part):
    field = base_field(jax.random.fold_in(key, 21))
    return field.astype(jnp.bfloat16)


def draw_keys(key, part):
    field = base_field(jax.random.fold_in(key, 22))
    return field.astype(jnp.bfloat16)


def block_levels(own_key, shape, shards, low, high):
    def one(dim, blocks):
        draws = jax.random.uniform(jax.random.fold_in(jax.random.fold_in(own_key, 6), dim), (blocks,), jnp.float32, low / len(shards), high / len(shards))
        return jnp.repeat(jnp.exp(draws), shape[dim] // blocks).reshape((-1,) + (1,) * (len(shape) - dim - 1))

    factor_of = one(*shards[0])
    for cut in shards[1:]:
        factor_of = factor_of * one(*cut)
    return factor_of


def noise(own_key, shape, scale, reach, shards=(), dtype=jnp.bfloat16):
    entries = jax.random.normal(own_key, shape, jnp.float32) * scale
    if len(shards) > 0:
        entries = block_levels(own_key, shape, shards, -0.22, 0.18) * entries
    return jnp.clip(entries, min=-reach, max=reach).astype(dtype)


def setup_inputs(seed: int = 0, part: int = 0) -> dict:
    arg_keys = jax.random.split(jax.random.key(seed), 7)
    own_keys = jax.random.split(jax.random.fold_in(arg_keys[6], part), 7)
    queries = draw_queries(jax.random.fold_in(jax.random.fold_in(arg_keys[6], part), 71), part)
    keys = draw_keys(jax.random.fold_in(jax.random.fold_in(arg_keys[6], part), 71), part)
    values = noise(own_keys[2], (TOKENS, HEADS * HDIM), 1.0, 6.0, ((0, 4), (1, 4)))
    d_out = noise(own_keys[3], (TOKENS, HEADS * HDIM), 1.0, 6.0, ((0, 4), (1, 4)))
    shift = jax.random.randint(own_keys[4], (1,), TOK_DEV // 4, 3 * TOK_DEV // 4 + 1).astype(jnp.int32)
    head_order = jax.random.permutation(arg_keys[5], HEADS).astype(jnp.int32)
    return {"queries": queries, "keys": keys, "values": values, "d_out": d_out, "shift": shift, "head_order": head_order}


def group_backward(qg, kg, vg, dg, allowed):
    scale = HDIM ** -0.5
    q32 = qg.astype(jnp.float32)
    k32 = kg.astype(jnp.float32)
    v32 = vg.astype(jnp.float32)
    d32 = dg.astype(jnp.float32)
    scores = jnp.einsum("gqd,gkd->gqk", q32, k32) * scale
    scores = jnp.where(allowed, scores, -1e30)
    top = jnp.max(scores, axis=-1, keepdims=True)
    weights = jnp.exp(scores - top)
    probs = weights / jnp.sum(weights, axis=-1, keepdims=True)
    probs_b = probs.astype(jnp.bfloat16).astype(jnp.float32)
    d_val = jnp.einsum("gqk,gqd->gkd", probs_b, d32)
    d_probs = jnp.einsum("gqd,gkd->gqk", d32, v32)
    row_dot = jnp.sum(probs * d_probs, axis=-1, keepdims=True)
    d_scores = (probs * (d_probs - row_dot)).astype(jnp.bfloat16).astype(jnp.float32)
    d_que = jnp.einsum("gqk,gkd->gqd", d_scores, k32) * scale
    d_key = jnp.einsum("gqk,gqd->gkd", d_scores, q32) * scale
    return d_que, d_key, d_val


def reference(queries, keys, values, d_out, shift, head_order):
    chosen = head_order[: HEADS // 2]
    every = jnp.arange(HEADS).astype(jnp.int32)
    flags = jnp.any(chosen[None, :] == every[:, None], axis=1)
    offsets = jnp.where(flags, shift[0], 0).astype(jnp.int32)
    places = jnp.arange(TOK_DEV)
    allowed = places[:, None] >= places[None, :]

    def one_head(index):
        off = offsets[index]
        start = (index * HDIM).astype(jnp.int32)
        parts = []
        for field in (queries, keys, values, d_out):
            piece = lax.dynamic_slice_in_dim(field, start, HDIM, 1)
            parts.append(jnp.roll(piece, -off, axis=0).reshape(TOKENS // TOK_DEV, TOK_DEV, HDIM))
        grads = group_backward(parts[0], parts[1], parts[2], parts[3], allowed)
        back = [jnp.roll(g.reshape(TOKENS, HDIM).astype(jnp.bfloat16), off, axis=0) for g in grads]
        return jnp.stack(back)

    stacked = lax.map(one_head, every)
    merged = jnp.transpose(stacked, (1, 2, 0, 3)).reshape(3, TOKENS, HEADS * HDIM)
    return (merged[0], merged[1], merged[2])
```

```python
import functools
import math

import jax
import jax.numpy as jnp
from jax import lax
from jax.experimental import pallas as pl
from jax.experimental.pallas import tpu as pltpu
from jax.sharding import PartitionSpec as P

HEADS = 32
HDIM = 128
SCALE = HDIM ** (-0.5)
LOG2_SCALE = SCALE * math.log2(math.e)
NEG = -1e30
GRAIN = 32
BLOCK = 256
F32 = jnp.float32
BF16 = jnp.bfloat16


def up(x, m):
    return (x + m - 1) // m * m


def dot_nt(a, b):
    return lax.dot_general(a, b, (((1,), (1,)), ((), ())), preferred_element_type=F32)


def dot_nn(a, b):
    return lax.dot_general(a, b, (((1,), (0,)), ((), ())), preferred_element_type=F32)


def dot_tn(a, b):
    return lax.dot_general(a, b, (((0,), (0,)), ((), ())), preferred_element_type=F32)


def query_blocks(rows):
    return [(q0, min(BLOCK, rows - q0)) for q0 in range(0, rows, BLOCK)]


def iotas(k0, kn, q0, w):
    key = k0 + lax.broadcasted_iota(jnp.int32, (kn, w), 0)
    query = q0 + lax.broadcasted_iota(jnp.int32, (1, w), 1)
    return key, query


def meta_kernel(heads, grain, caps, shift_ref, order_ref, out_ref, flag_ref):
    base = lax.axis_index("head") * heads
    for h in range(heads):
        flag_ref[h] = 0
    for i in range(HEADS // 2):
        loc = order_ref[i] - base

        @pl.when((loc >= 0) & (loc < heads))
        def _():
            flag_ref[loc] = 1

    count = flag_ref[0]
    for h in range(1, heads):
        count = count + flag_ref[h]
    yes, no = jnp.int32(0), count
    for h in range(heads):
        flag = flag_ref[h]
        out_ref[jnp.where(flag > 0, yes, no)] = h
        yes, no = yes + flag, no + 1 - flag
    off = shift_ref[0]
    slot = (off + grain - 1) // grain * grain
    pick = jnp.where(count > 0, 1, 0)
    for cap in caps[:-1]:
        pick = pick + jnp.where(count * slot > cap, 1, 0)
    out_ref[heads] = count
    out_ref[heads + 1] = off
    out_ref[heads + 2] = slot
    out_ref[heads + 3] = pick


def shifted_at(heads):
    return lambda s, m: m[jnp.minimum(s, m[heads] - 1)]


def pack_kernel(heads, meta, q_ref, d_ref, out_ref):
    s = pl.program_id(0)
    count, slot = meta[heads], meta[heads + 2]

    @pl.when(s == 0)
    def _():
        out_ref[...] = jnp.zeros_like(out_ref)

    @pl.when(s < count)
    def _():
        def step(i, c):
            src = pl.multiple_of(i * GRAIN, GRAIN)
            dst = pl.multiple_of(s * slot + i * GRAIN, GRAIN)
            out_ref[pl.ds(dst, GRAIN), :HDIM] = q_ref[pl.ds(src, GRAIN), :]
            out_ref[pl.ds(dst, GRAIN), HDIM:] = d_ref[pl.ds(src, GRAIN), :]
            return c

        lax.fori_loop(0, slot // GRAIN, step, 0)


def stats_kernel(heads, rows, reach, meta, q_ref, k_ref, v_ref, d_ref, send_ref, own_ref):
    s = pl.program_id(0)

    @pl.when(s < meta[heads])
    def _():
        off = meta[heads + 1]
        for q0, w in query_blocks(rows):
            kn = q0 + w
            key, query = iotas(0, kn, q0, w)
            low = jnp.where(query >= off, off, 0)
            sc = dot_nt(k_ref[:kn, :], q_ref[q0:kn, :]) * LOG2_SCALE
            sc = jnp.where((key <= query) & (key >= low), sc, NEG)
            top = jnp.max(sc, axis=0, keepdims=True)
            e = jnp.exp2(sc - top)
            total = jnp.sum(e, axis=0, keepdims=True)
            dp = dot_nt(v_ref[:kn, :], d_ref[q0:kn, :])
            rd = jnp.sum(e * dp, axis=0, keepdims=True) / total
            lse = top + jnp.log2(total)
            own_ref[s, 0:1, q0:kn] = lse
            own_ref[s, 1:2, q0:kn] = rd
            if q0 < reach:
                send_ref[s, 0:1, q0:kn] = lse
                send_ref[s, 1:2, q0:kn] = rd


def plain_kernel(heads, rows, meta, q_ref, k_ref, v_ref, d_ref, dq_ref, dk_ref, dv_ref, ak_ref, av_ref):
    s = pl.program_id(0)

    @pl.when(s >= meta[heads])
    def _():
        for q0, w in query_blocks(rows):
            kn = q0 + w
            qb, db = q_ref[q0:kn, :], d_ref[q0:kn, :]
            parts = ([(0, q0, False)] if q0 else []) + [(q0, w, True)]
            scores = []
            for k0, n, diagonal in parts:
                sc = dot_nt(k_ref[k0 : k0 + n, :], qb) * LOG2_SCALE
                if diagonal:
                    key, query = iotas(k0, n, q0, w)
                    sc = jnp.where(key <= query, sc, NEG)
                scores.append(sc)
            tops = [jnp.max(sc, axis=0, keepdims=True) for sc in scores]
            top = functools.reduce(jnp.maximum, tops)
            es = [jnp.exp2(sc - top) for sc in scores]
            total = sum(jnp.sum(e, axis=0, keepdims=True) for e in es)
            dps = [dot_nt(v_ref[k0 : k0 + n, :], db) for k0, n, _ in parts]
            inv = 1.0 / total
            rd = sum(jnp.sum(e * dp, axis=0, keepdims=True) for e, dp in zip(es, dps)) * inv
            dq = None
            for (k0, n, diagonal), e, dp in zip(parts, es, dps):
                p = e * inv
                ds = (p * (dp - rd)).astype(BF16)
                gv = dot_nn(p.astype(BF16), db)
                gk = dot_nn(ds, qb)
                gq = dot_tn(ds, k_ref[k0 : k0 + n, :])
                dq = gq if dq is None else dq + gq
                if diagonal:
                    av_ref[k0 : k0 + n, :] = gv
                    ak_ref[k0 : k0 + n, :] = gk
                else:
                    av_ref[k0 : k0 + n, :] += gv
                    ak_ref[k0 : k0 + n, :] += gk
            dq_ref[q0:kn, :] = (dq * SCALE).astype(BF16)
        dk_ref[...] = (ak_ref[...] * SCALE).astype(BF16)
        dv_ref[...] = av_ref[...].astype(BF16)


def cross_kernel(
    heads, rows, first, reach, cap, meta, k_ref, v_ref, got_ref, st_ref,
    back_ref, tot_ref, gk_ref, gv_ref, buf_ref, acc_ref,
):
    s = pl.program_id(0)
    count, off, slot = meta[heads], meta[heads + 1], meta[heads + 2]
    kn = rows - first

    @pl.when(s == 0)
    def _():
        buf_ref[cap:, :] = jnp.zeros((buf_ref.shape[0] - cap, 2 * HDIM), BF16)
        pltpu.sync_copy(got_ref, buf_ref.at[pl.ds(0, cap), :])
        acc_ref[...] = jnp.zeros_like(acc_ref)

    def block(q0, fresh):
        start = pl.multiple_of(s * slot + q0, GRAIN)
        qb = buf_ref[pl.ds(start, BLOCK), :HDIM]
        db = buf_ref[pl.ds(start, BLOCK), HDIM:]
        kb, vb = k_ref[first:, :], v_ref[first:, :]
        key, query = iotas(first, kn, q0, BLOCK)
        inside = query < off
        sc = dot_nt(kb, qb) * LOG2_SCALE
        sc = jnp.where(key >= off, sc, NEG)
        top = jnp.max(sc, axis=0, keepdims=True)
        e = jnp.exp2(sc - top)
        total = jnp.sum(e, axis=0, keepdims=True)
        dp = dot_nt(vb, db)
        rd = jnp.sum(e * dp, axis=0, keepdims=True) / total
        lse = top + jnp.log2(total)
        lse1 = jnp.where(inside, st_ref[s, 0:1, q0 : q0 + BLOCK], 0.0)
        rd1 = jnp.where(inside, st_ref[s, 1:2, q0 : q0 + BLOCK], 0.0)
        high = jnp.maximum(lse, lse1)
        both = high + jnp.log2(jnp.exp2(lse - high) + jnp.exp2(lse1 - high))
        rd = jnp.exp2(lse - both) * rd + jnp.exp2(lse1 - both) * rd1
        tot_ref[s, 0:1, q0 : q0 + BLOCK] = both
        tot_ref[s, 1:2, q0 : q0 + BLOCK] = rd
        p = e * jnp.where(inside, jnp.exp2(top - both), 0.0)
        ds = (p * (dp - rd)).astype(BF16)
        gv = dot_nn(p.astype(BF16), db)
        gk = dot_nn(ds, qb)
        gq = dot_tn(ds, kb) * SCALE
        acc_ref[pl.ds(start, BLOCK), :] = gq.astype(BF16)
        if fresh:
            gv_ref[0] = gv
            gk_ref[0] = gk
        else:
            gv_ref[0] += gv
            gk_ref[0] += gk

    for q0 in range(0, reach, BLOCK):

        @pl.when((s < count) & (off > q0))
        def _(q0=q0):
            block(q0, q0 == 0)

    @pl.when(s == pl.num_programs(0) - 1)
    def _():
        back_ref[...] = acc_ref[:cap, :]


def local_kernel(
    heads, rows, first, reach, meta, q_ref, k_ref, v_ref, d_ref, own_ref, tot_ref, gk_ref, gv_ref,
    _dq, _dk, _dv, dq_ref, dk_ref, dv_ref, ak_ref, av_ref,
):
    s = pl.program_id(0)

    @pl.when(s < meta[heads])
    def _():
        off = meta[heads + 1]
        for q0, w in query_blocks(rows):
            kn = q0 + w
            key, query = iotas(0, kn, q0, w)
            low = jnp.where(query >= off, off, 0)
            lse = own_ref[s, 0:1, q0:kn]
            rd = own_ref[s, 1:2, q0:kn]
            if q0 < reach:
                lse = jnp.where(query < off, tot_ref[s, 0:1, q0:kn], lse)
                rd = jnp.where(query < off, tot_ref[s, 1:2, q0:kn], rd)
            qb, db = q_ref[q0:kn, :], d_ref[q0:kn, :]
            sc = dot_nt(k_ref[:kn, :], qb) * LOG2_SCALE
            p = jnp.where((key <= query) & (key >= low), jnp.exp2(sc - lse), 0.0)
            dp = dot_nt(v_ref[:kn, :], db)
            ds = (p * (dp - rd)).astype(BF16)
            gv = dot_nn(p.astype(BF16), db)
            gk = dot_nn(ds, qb)
            dq_ref[q0:kn, :] = (dot_tn(ds, k_ref[:kn, :]) * SCALE).astype(BF16)
            if q0:
                av_ref[:q0, :] += gv[:q0]
                ak_ref[:q0, :] += gk[:q0]
            av_ref[q0:kn, :] = gv[q0:]
            ak_ref[q0:kn, :] = gk[q0:]
        dk_ref[:first, :] = (ak_ref[:first, :] * SCALE).astype(BF16)
        dv_ref[:first, :] = av_ref[:first, :].astype(BF16)
        dk_ref[first:, :] = ((ak_ref[first:, :] + gk_ref[0]) * SCALE).astype(BF16)
        dv_ref[first:, :] = (av_ref[first:, :] + gv_ref[0]).astype(BF16)


def add_kernel(heads, meta, got_ref, in_ref, out_ref):
    s = pl.program_id(0)
    slot = meta[heads + 2]

    @pl.when(s < meta[heads])
    def _():
        out_ref[...] = in_ref[...]

        def step(i, c):
            dst = pl.multiple_of(i * GRAIN, GRAIN)
            src = pl.multiple_of(s * slot + i * GRAIN, GRAIN)
            here = in_ref[pl.ds(dst, GRAIN), :].astype(F32)
            there = got_ref[pl.ds(src, GRAIN), :].astype(F32)
            out_ref[pl.ds(dst, GRAIN), :] = (here + there).astype(BF16)
            return c

        lax.fori_loop(0, slot // GRAIN, step, 0)


def cost(flops, moved):
    return pl.CostEstimate(flops=int(flops), bytes_accessed=int(moved), transcendentals=0)


def shards(queries, keys, values, d_out, shift, head_order):
    rows, width = queries.shape
    heads = width // HDIM
    first, last = rows // 4, rows - rows // 4
    tallest = up(last, GRAIN)
    reach = up(last, BLOCK)
    most = heads * tallest
    fractions = (0.17, 0.26, 0.35, 0.44, 0.54, 0.67, 0.83, 1.0)
    caps = [up(int(most * f), GRAIN) for f in fractions]
    seq = lax.axis_size("seq")
    back = [(i, (i - 1) % seq) for i in range(seq)]
    ahead = [(i, (i + 1) % seq) for i in range(seq)]

    meta = pl.pallas_call(
        functools.partial(meta_kernel, heads, GRAIN, caps),
        out_shape=jax.ShapeDtypeStruct((heads + 4,), jnp.int32),
        in_specs=[pl.BlockSpec(memory_space=pltpu.SMEM)] * 2,
        out_specs=pl.BlockSpec(memory_space=pltpu.SMEM),
        scratch_shapes=[pltpu.SMEM((heads,), jnp.int32)],
        name="meta",
    )(shift, head_order)

    at = shifted_at(heads)
    whole = jax.ShapeDtypeStruct((rows, width), BF16)
    head_spec = pl.BlockSpec((rows, HDIM), lambda s, m: (0, at(s, m)))
    plain_at = lambda s, m: m[jnp.minimum(jnp.maximum(s, m[heads]), heads - 1)]
    plain_spec = pl.BlockSpec((rows, HDIM), lambda s, m: (0, plain_at(s, m)))
    any_spec = pl.BlockSpec(memory_space=pl.ANY)
    tile = rows * HDIM * 2
    work = 2 * rows * rows * HDIM

    def full(*shape):
        return pl.BlockSpec(shape, lambda s, m: (0,) * len(shape))

    def call(kernel, name, in_specs, out_specs, out_shape, estimate, scratch=(), aliases={}):
        return pl.pallas_call(
            kernel,
            out_shape=out_shape,
            grid_spec=pltpu.PrefetchScalarGridSpec(
                num_scalar_prefetch=1,
                grid=(heads,),
                in_specs=in_specs,
                out_specs=out_specs,
                scratch_shapes=list(scratch),
            ),
            input_output_aliases=aliases,
            cost_estimate=estimate,
            name=name,
        )

    def plain(meta, queries, keys, values, d_out):
        return call(
            functools.partial(plain_kernel, heads, rows),
            "plain",
            [plain_spec] * 4,
            [plain_spec] * 3,
            [whole] * 3,
            cost(heads / 2 * 4 * work, heads / 2 * 7 * tile),
            [pltpu.VMEM((rows, HDIM), F32)] * 2,
        )(meta, queries, keys, values, d_out)

    def branch(cap):
        def run(meta, queries, keys, values, d_out):
            top_spec = pl.BlockSpec((tallest, HDIM), lambda s, m: (0, at(s, m)))
            sent = call(
                functools.partial(pack_kernel, heads),
                "pack",
                [top_spec] * 2,
                full(cap, 2 * HDIM),
                jax.ShapeDtypeStruct((cap, 2 * HDIM), BF16),
                cost(0, 2 * cap * HDIM * 4),
            )(meta, queries, d_out)
            got = lax.ppermute(sent, "seq", back)
            st_send, st_own = call(
                functools.partial(stats_kernel, heads, rows, reach),
                "stats",
                [head_spec] * 4,
                [full(heads, 2, reach), full(heads, 2, rows)],
                [
                    jax.ShapeDtypeStruct((heads, 2, reach), F32),
                    jax.ShapeDtypeStruct((heads, 2, rows), F32),
                ],
                cost(heads / 2 * 2 * work, heads / 2 * 4 * tile),
            )(meta, queries, keys, values, d_out)
            st_got = lax.ppermute(st_send, "seq", back)
            dq, dk, dv = plain(meta, queries, keys, values, d_out)
            side = jax.ShapeDtypeStruct((heads, rows - first, HDIM), F32)
            side_spec = pl.BlockSpec((1, rows - first, HDIM), lambda s, m: (jnp.minimum(s, m[heads] - 1), 0, 0))
            back_q, tot, gk, gv = call(
                functools.partial(cross_kernel, heads, rows, first, reach, cap),
                "cross",
                [head_spec] * 2 + [any_spec, full(heads, 2, reach)],
                [full(cap, HDIM), full(heads, 2, reach), side_spec, side_spec],
                [
                    jax.ShapeDtypeStruct((cap, HDIM), BF16),
                    jax.ShapeDtypeStruct((heads, 2, reach), F32),
                    side,
                    side,
                ],
                cost(heads / 2 * 5 * work, heads / 2 * 6 * tile),
                [pltpu.VMEM((cap + BLOCK, 2 * HDIM), BF16), pltpu.VMEM((cap + BLOCK, HDIM), BF16)],
            )(meta, keys, values, got, st_got)
            tot_got = lax.ppermute(tot, "seq", ahead)
            dq_got = lax.ppermute(back_q, "seq", ahead)
            dq, dk, dv = call(
                functools.partial(local_kernel, heads, rows, first, reach),
                "local",
                [head_spec] * 4
                + [full(heads, 2, rows), full(heads, 2, reach), side_spec, side_spec]
                + [any_spec] * 3,
                [head_spec] * 3,
                [whole] * 3,
                cost(heads / 2 * 4 * work, heads / 2 * 9 * tile),
                [pltpu.VMEM((rows, HDIM), F32)] * 2,
                {9: 0, 10: 1, 11: 2},
            )(meta, queries, keys, values, d_out, st_own, tot_got, gk, gv, dq, dk, dv)
            dq = call(
                functools.partial(add_kernel, heads),
                "add",
                [full(cap, HDIM), top_spec],
                top_spec,
                whole,
                cost(0, heads / 2 * 3 * tile),
                aliases={2: 0},
            )(meta, dq_got, dq)
            return dq, dk, dv

        return run

    return tuple(
        lax.switch(
            meta[heads + 3],
            [plain] + [branch(cap) for cap in caps],
            meta,
            queries,
            keys,
            values,
            d_out,
        )
    )


def solution(mesh):
    spec = P(("rep", "seq"), "head")
    return jax.shard_map(
        shards,
        mesh=mesh,
        in_specs=(spec, spec, spec, spec, P("rep"), P()),
        out_specs=(spec, spec, spec),
        check_vma=False,
    )
```

```python
import functools
import math

import jax
import jax.numpy as jnp
from jax import lax
from jax.experimental import pallas as pl
from jax.experimental.pallas import tpu as pltpu
from jax.sharding import PartitionSpec as P


HEADS = 32
HDIM = 128
SCALE = HDIM ** (-0.5)
LOG2_SCALE = SCALE * math.log2(math.e)
NEG = -1e30
GRAIN = 32
BLOCK = 256
F32 = jnp.float32
BF16 = jnp.bfloat16


def up(x, m):
    return (x + m - 1) // m * m


def dot_nt(a, b):
    return lax.dot_general(a, b, (((1,), (1,)), ((), ())), preferred_element_type=F32)


def dot_nn(a, b):
    return lax.dot_general(a, b, (((1,), (0,)), ((), ())), preferred_element_type=F32)


def dot_tn(a, b):
    return lax.dot_general(a, b, (((0,), (0,)), ((), ())), preferred_element_type=F32)


def query_blocks(rows):
    return [(q0, min(BLOCK, rows - q0)) for q0 in range(0, rows, BLOCK)]


def iotas(k0, kn, q0, w):
    key = k0 + lax.broadcasted_iota(jnp.int32, (kn, w), 0)
    query = q0 + lax.broadcasted_iota(jnp.int32, (1, w), 1)
    return key, query


def meta_kernel(heads, grain, caps, shift_ref, order_ref, out_ref, flag_ref):
    base = lax.axis_index("head") * heads
    for h in range(heads):
        flag_ref[h] = 0
    for i in range(HEADS // 2):
        loc = order_ref[i] - base

        @pl.when((loc >= 0) & (loc < heads))
        def _():
            flag_ref[loc] = 1

    count = flag_ref[0]
    for h in range(1, heads):
        count = count + flag_ref[h]
    yes, no = jnp.int32(0), count
    for h in range(heads):
        flag = flag_ref[h]
        out_ref[jnp.where(flag > 0, yes, no)] = h
        yes, no = yes + flag, no + 1 - flag
    off = shift_ref[0]
    slot = (off + grain - 1) // grain * grain
    pick = jnp.where(count > 0, 1, 0)
    for cap in caps[:-1]:
        pick = pick + jnp.where(count * slot > cap, 1, 0)
    out_ref[heads] = count
    out_ref[heads + 1] = off
    out_ref[heads + 2] = slot
    out_ref[heads + 3] = pick


def shifted_at(heads):
    return lambda s, m: m[jnp.minimum(s, m[heads] - 1)]


def pack_kernel(heads, base, sizes, meta, q_ref, d_ref, out_ref, sem):
    count, slot = meta[heads], meta[heads + 2]

    def each(act):
        def step(s, c):
            column = pl.multiple_of(meta[s] * HDIM, HDIM)

            def copy(at, size, i):
                src = pl.multiple_of(at, GRAIN)
                dst = pl.multiple_of(s * slot + at, GRAIN)
                for j, ref in enumerate((q_ref, d_ref)):
                    act(
                        pltpu.make_async_copy(
                            ref.at[pl.ds(src, size), pl.ds(column, HDIM)],
                            out_ref.at[pl.ds(dst, size), pl.ds(j * HDIM, HDIM)],
                            sem.at[s, j, i],
                        )
                    )

            copy(0, base, 0)
            at = jnp.int32(base)
            for i, size in enumerate(sizes):
                bit = ((slot - base) // size) % 2

                @pl.when(bit == 1)
                def _(at=at, size=size, i=i):
                    copy(at, size, i + 1)

                at = at + bit * size
            return c

        lax.fori_loop(0, count, step, 0)

    each(lambda copy: copy.start())
    each(lambda copy: copy.wait())


def stats_kernel(heads, rows, reach, meta, q_ref, k_ref, v_ref, d_ref, send_ref, own_ref):
    s = pl.program_id(0)

    @pl.when(s < meta[heads])
    def _():
        off = meta[heads + 1]
        for q0, w in query_blocks(rows):
            kn = q0 + w
            key, query = iotas(0, kn, q0, w)
            low = jnp.where(query >= off, off, 0)
            sc = dot_nt(k_ref[:kn, :], q_ref[q0:kn, :]) * LOG2_SCALE
            sc = jnp.where((key <= query) & (key >= low), sc, NEG)
            top = jnp.max(sc, axis=0, keepdims=True)
            e = jnp.exp2(sc - top)
            total = jnp.sum(e, axis=0, keepdims=True)
            dp = dot_nt(v_ref[:kn, :], d_ref[q0:kn, :])
            rd = jnp.sum(e * dp, axis=0, keepdims=True) / total
            lse = top + jnp.log2(total)
            own_ref[s, 0:1, q0:kn] = lse
            own_ref[s, 1:2, q0:kn] = rd
            if q0 < reach:
                send_ref[s, 0:1, q0:kn] = lse
                send_ref[s, 1:2, q0:kn] = rd


def plain_kernel(heads, rows, meta, q_ref, k_ref, v_ref, d_ref, dq_ref, dk_ref, dv_ref, ak_ref, av_ref):
    s = pl.program_id(0)

    @pl.when(s >= meta[heads])
    def _():
        for q0, w in query_blocks(rows):
            kn = q0 + w
            qb, db = q_ref[q0:kn, :], d_ref[q0:kn, :]
            parts = ([(0, q0, False)] if q0 else []) + [(q0, w, True)]
            scores = []
            for k0, n, diagonal in parts:
                sc = dot_nt(k_ref[k0 : k0 + n, :], qb) * LOG2_SCALE
                if diagonal:
                    key, query = iotas(k0, n, q0, w)
                    sc = jnp.where(key <= query, sc, NEG)
                scores.append(sc)
            tops = [jnp.max(sc, axis=0, keepdims=True) for sc in scores]
            top = functools.reduce(jnp.maximum, tops)
            es = [jnp.exp2(sc - top) for sc in scores]
            total = sum(jnp.sum(e, axis=0, keepdims=True) for e in es)
            dps = [dot_nt(v_ref[k0 : k0 + n, :], db) for k0, n, _ in parts]
            inv = 1.0 / total
            rd = sum(jnp.sum(e * dp, axis=0, keepdims=True) for e, dp in zip(es, dps)) * inv
            dq = None
            for (k0, n, diagonal), e, dp in zip(parts, es, dps):
                p = e * inv
                ds = (p * (dp - rd)).astype(BF16)
                gv = dot_nn(p.astype(BF16), db)
                gk = dot_nn(ds, qb)
                gq = dot_tn(ds, k_ref[k0 : k0 + n, :])
                dq = gq if dq is None else dq + gq
                if diagonal:
                    av_ref[k0 : k0 + n, :] = gv
                    ak_ref[k0 : k0 + n, :] = gk
                else:
                    av_ref[k0 : k0 + n, :] += gv
                    ak_ref[k0 : k0 + n, :] += gk
            dq_ref[q0:kn, :] = (dq * SCALE).astype(BF16)
        dk_ref[...] = (ak_ref[...] * SCALE).astype(BF16)
        dv_ref[...] = av_ref[...].astype(BF16)


def cross_kernel(
    heads, rows, first, meta, k_ref, v_ref, got_ref, st_ref, _after,
    back_ref, tot_ref, gk_ref, gv_ref, buf_ref, acc_ref,
):
    s = pl.program_id(0)
    count, off, slot = meta[heads], meta[heads + 1], meta[heads + 2]
    filled = count * slot

    @pl.when(s == 0)
    def _():
        def step(i, c):
            at = pl.multiple_of(i * GRAIN, GRAIN)
            buf_ref[pl.ds(at, GRAIN), :] = got_ref[pl.ds(at, GRAIN), :]
            return c

        lax.fori_loop(0, filled // GRAIN, step, 0)
        tail = pl.multiple_of(filled, GRAIN)
        buf_ref[pl.ds(tail, BLOCK), :] = jnp.zeros((BLOCK, 2 * HDIM), BF16)

    def block(j, k0):
        q0 = pl.multiple_of(j * BLOCK, BLOCK)
        start = pl.multiple_of(s * slot + q0, GRAIN)
        qb = buf_ref[pl.ds(start, BLOCK), :HDIM]
        db = buf_ref[pl.ds(start, BLOCK), HDIM:]
        kb, vb = k_ref[k0:, :], v_ref[k0:, :]
        key = k0 + lax.broadcasted_iota(jnp.int32, (rows - k0, BLOCK), 0)
        query = q0 + lax.broadcasted_iota(jnp.int32, (1, BLOCK), 1)
        inside = query < off
        sc = dot_nt(kb, qb) * LOG2_SCALE
        sc = jnp.where(key >= off, sc, NEG)
        top = jnp.max(sc, axis=0, keepdims=True)
        e = jnp.exp2(sc - top)
        total = jnp.sum(e, axis=0, keepdims=True)
        dp = dot_nt(vb, db)
        rd = jnp.sum(e * dp, axis=0, keepdims=True) / total
        lse = top + jnp.log2(total)
        lse1 = jnp.where(inside, st_ref[s, 0:1, pl.ds(q0, BLOCK)], 0.0)
        rd1 = jnp.where(inside, st_ref[s, 1:2, pl.ds(q0, BLOCK)], 0.0)
        high = jnp.maximum(lse, lse1)
        both = high + jnp.log2(jnp.exp2(lse - high) + jnp.exp2(lse1 - high))
        rd = jnp.exp2(lse - both) * rd + jnp.exp2(lse1 - both) * rd1
        tot_ref[s, 0:1, pl.ds(q0, BLOCK)] = both
        tot_ref[s, 1:2, pl.ds(q0, BLOCK)] = rd
        p = e * jnp.where(inside, jnp.exp2(top - both), 0.0)
        ds = (p * (dp - rd)).astype(BF16)
        gv_ref[s, k0 - first :, :] += dot_nn(p.astype(BF16), db)
        gk_ref[s, k0 - first :, :] += dot_nn(ds, qb)
        acc_ref[pl.ds(start, BLOCK), :] = (dot_tn(ds, kb) * SCALE).astype(BF16)

    @pl.when(s < count)
    def _():
        gv_ref[s] = jnp.zeros(gv_ref.shape[1:], F32)
        gk_ref[s] = jnp.zeros(gk_ref.shape[1:], F32)
        starts = (first, up(2 * first, GRAIN))
        blocks = (off + BLOCK - 1) // BLOCK
        for k0, mine in ((starts[0], off < starts[1]), (starts[1], off >= starts[1])):

            @pl.when(mine)
            def _(k0=k0):
                def step(j, c):
                    block(j, k0)
                    return c

                lax.fori_loop(0, blocks, step, 0)

    @pl.when(s == pl.num_programs(0) - 1)
    def _():
        def step(i, c):
            at = pl.multiple_of(i * GRAIN, GRAIN)
            back_ref[pl.ds(at, GRAIN), :] = acc_ref[pl.ds(at, GRAIN), :]
            return c

        lax.fori_loop(0, filled // GRAIN, step, 0)


def local_kernel(
    heads, rows, first, reach, meta, q_ref, k_ref, v_ref, d_ref, own_ref, tot_ref, gk_ref, gv_ref,
    _dq, _dk, _dv, dq_ref, dk_ref, dv_ref, part_ref, ak_ref, av_ref,
):
    s = pl.program_id(0)

    @pl.when(s < meta[heads])
    def _():
        off = meta[heads + 1]
        for q0, w in query_blocks(rows):
            kn = q0 + w
            key, query = iotas(0, kn, q0, w)
            low = jnp.where(query >= off, off, 0)
            lse = own_ref[s, 0:1, q0:kn]
            rd = own_ref[s, 1:2, q0:kn]
            if q0 < reach:
                lse = jnp.where(query < off, tot_ref[s, 0:1, q0:kn], lse)
                rd = jnp.where(query < off, tot_ref[s, 1:2, q0:kn], rd)
            qb, db = q_ref[q0:kn, :], d_ref[q0:kn, :]
            sc = dot_nt(k_ref[:kn, :], qb) * LOG2_SCALE
            p = jnp.where((key <= query) & (key >= low), jnp.exp2(sc - lse), 0.0)
            dp = dot_nt(v_ref[:kn, :], db)
            ds = (p * (dp - rd)).astype(BF16)
            gv = dot_nn(p.astype(BF16), db)
            gk = dot_nn(ds, qb)
            dq = dot_tn(ds, k_ref[:kn, :]) * SCALE
            dq_ref[q0:kn, :] = dq.astype(BF16)
            if q0 < reach:
                part_ref[s, q0:kn, :] = dq
            if q0:
                av_ref[:q0, :] += gv[:q0]
                ak_ref[:q0, :] += gk[:q0]
            av_ref[q0:kn, :] = gv[q0:]
            ak_ref[q0:kn, :] = gk[q0:]
        dk_ref[:first, :] = (ak_ref[:first, :] * SCALE).astype(BF16)
        dv_ref[:first, :] = av_ref[:first, :].astype(BF16)
        dk_ref[first:, :] = ((ak_ref[first:, :] + gk_ref[s]) * SCALE).astype(BF16)
        dv_ref[first:, :] = (av_ref[first:, :] + gv_ref[s]).astype(BF16)


def add_kernel(heads, tallest, meta, part_ref, got_ref, _dq, dq_ref, stage_ref, sem):
    slot = meta[heads + 2]

    def copy(s):
        column = pl.multiple_of(meta[s] * HDIM, HDIM)
        return pltpu.make_async_copy(
            stage_ref.at[s], dq_ref.at[pl.ds(0, tallest), pl.ds(column, HDIM)], sem.at[s]
        )

    def send(s, c):
        def both(i, c):
            at = pl.multiple_of(i * GRAIN, GRAIN)
            src = pl.multiple_of(s * slot + i * GRAIN, GRAIN)
            there = got_ref[pl.ds(src, GRAIN), :].astype(F32)
            stage_ref[s, pl.ds(at, GRAIN), :] = (part_ref[s, pl.ds(at, GRAIN), :] + there).astype(BF16)
            return c

        def here(i, c):
            at = pl.multiple_of(i * GRAIN, GRAIN)
            stage_ref[s, pl.ds(at, GRAIN), :] = part_ref[s, pl.ds(at, GRAIN), :].astype(BF16)
            return c

        lax.fori_loop(0, slot // GRAIN, both, 0)
        lax.fori_loop(slot // GRAIN, tallest // GRAIN, here, 0)
        copy(s).start()
        return c

    def wait(s, c):
        copy(s).wait()
        return c

    lax.fori_loop(0, meta[heads], send, 0)
    lax.fori_loop(0, meta[heads], wait, 0)


def cost(flops, moved):
    return pl.CostEstimate(flops=int(flops), bytes_accessed=int(moved), transcendentals=0)


def shards(queries, keys, values, d_out, shift, head_order):
    rows, width = queries.shape
    heads = width // HDIM
    first, last = rows // 4, rows - rows // 4
    base = first // GRAIN * GRAIN
    tallest = up(last, GRAIN)
    reach = up(last, BLOCK)
    most = heads * tallest
    fractions = (0.25, 0.38, 0.5, 0.67, 1.0)
    caps = [up(int(most * f), GRAIN) for f in fractions]
    seq = lax.axis_size("seq")
    back = [(i, (i - 1) % seq) for i in range(seq)]
    ahead = [(i, (i + 1) % seq) for i in range(seq)]

    meta = pl.pallas_call(
        functools.partial(meta_kernel, heads, GRAIN, caps),
        out_shape=jax.ShapeDtypeStruct((heads + 4,), jnp.int32),
        in_specs=[pl.BlockSpec(memory_space=pltpu.SMEM)] * 2,
        out_specs=pl.BlockSpec(memory_space=pltpu.SMEM),
        scratch_shapes=[pltpu.SMEM((heads,), jnp.int32)],
        name="meta",
    )(shift, head_order)

    at = shifted_at(heads)
    whole = jax.ShapeDtypeStruct((rows, width), BF16)
    head_spec = pl.BlockSpec((rows, HDIM), lambda s, m: (0, at(s, m)))
    plain_at = lambda s, m: m[jnp.minimum(jnp.maximum(s, m[heads]), heads - 1)]
    plain_spec = pl.BlockSpec((rows, HDIM), lambda s, m: (0, plain_at(s, m)))
    any_spec = pl.BlockSpec(memory_space=pl.ANY)
    vmem = pl.BlockSpec(memory_space=pltpu.VMEM)
    smem = pl.BlockSpec(memory_space=pltpu.SMEM)
    tile = rows * HDIM * 2
    work = 2 * rows * rows * HDIM

    def call(kernel, in_specs, out_specs, out_shape, estimate, scratch=(), aliases={}):
        return pl.pallas_call(
            kernel,
            out_shape=out_shape,
            grid_spec=pltpu.PrefetchScalarGridSpec(
                num_scalar_prefetch=1,
                grid=(heads,),
                in_specs=in_specs,
                out_specs=out_specs,
                scratch_shapes=list(scratch),
            ),
            input_output_aliases=aliases,
            cost_estimate=estimate,
        )

    def plain(meta, queries, keys, values, d_out):
        return call(
            functools.partial(plain_kernel, heads, rows),
            [plain_spec] * 4,
            [plain_spec] * 3,
            [whole] * 3,
            cost(heads / 2 * 4 * work, heads / 2 * 7 * tile),
            [pltpu.VMEM((rows, HDIM), F32)] * 2,
        )(meta, queries, keys, values, d_out)

    def branch(cap):
        def steps(meta, queries, keys, values, d_out):
            sizes, left = [], tallest - base
            while sum(sizes) < left:
                sizes.append(GRAIN * 2 ** len(sizes))
            sent = pl.pallas_call(
                functools.partial(pack_kernel, heads, base, sizes),
                out_shape=jax.ShapeDtypeStruct((cap, 2 * HDIM), BF16),
                in_specs=[smem, any_spec, any_spec],
                out_specs=vmem,
                scratch_shapes=[pltpu.SemaphoreType.DMA((heads, 2, 1 + len(sizes)))],
                cost_estimate=cost(0, 2 * cap * HDIM * 4),
                name="pack",
            )(meta, queries, d_out)
            got = lax.ppermute(sent, "seq", back)
            st_send, st_own = call(
                functools.partial(stats_kernel, heads, rows, reach),
                [head_spec] * 4,
                [vmem, vmem],
                [
                    jax.ShapeDtypeStruct((heads, 2, reach), F32),
                    jax.ShapeDtypeStruct((heads, 2, rows), F32),
                ],
                cost(heads / 2 * 2 * work, heads / 2 * 4 * tile),
            )(meta, queries, keys, values, d_out)
            st_got = lax.ppermute(st_send, "seq", back)
            dq, dk, dv = plain(meta, queries, keys, values, d_out)
            side = jax.ShapeDtypeStruct((heads, rows - first, HDIM), F32)
            back_q, tot, gk, gv = call(
                functools.partial(cross_kernel, heads, rows, first),
                [head_spec] * 2 + [vmem, vmem, any_spec],
                [vmem] * 4,
                [
                    jax.ShapeDtypeStruct((cap, HDIM), BF16),
                    jax.ShapeDtypeStruct((heads, 2, reach), F32),
                    side,
                    side,
                ],
                cost(heads / 2 * 5 * work, heads / 2 * 6 * tile),
                [pltpu.VMEM((cap + BLOCK, 2 * HDIM), BF16), pltpu.VMEM((cap + BLOCK, HDIM), BF16)],
            )(meta, keys, values, got, st_got, dq)
            tot_got = lax.ppermute(tot, "seq", ahead)
            dq_got = lax.ppermute(back_q, "seq", ahead)
            dq, dk, dv, part = call(
                functools.partial(local_kernel, heads, rows, first, reach),
                [head_spec] * 4
                + [vmem] * 4
                + [any_spec] * 3,
                [head_spec] * 3 + [vmem],
                [whole] * 3 + [jax.ShapeDtypeStruct((heads, reach, HDIM), F32)],
                cost(heads / 2 * 4 * work, heads / 2 * 9 * tile),
                [pltpu.VMEM((rows, HDIM), F32)] * 2,
                {9: 0, 10: 1, 11: 2},
            )(meta, queries, keys, values, d_out, st_own, tot_got, gk, gv, dq, dk, dv)
            dq = pl.pallas_call(
                functools.partial(add_kernel, heads, tallest),
                out_shape=whole,
                in_specs=[smem, vmem, vmem, any_spec],
                out_specs=any_spec,
                scratch_shapes=[
                    pltpu.VMEM((heads, tallest, HDIM), BF16),
                    pltpu.SemaphoreType.DMA((heads,)),
                ],
                input_output_aliases={3: 0},
                cost_estimate=cost(0, heads / 2 * 3 * tile),
                name="add",
            )(meta, part, dq_got, dq)
            return dq, dk, dv

        return steps

    return tuple(
        lax.switch(
            meta[heads + 3],
            [plain] + [branch(cap) for cap in caps],
            meta,
            queries,
            keys,
            values,
            d_out,
        )
    )


def solution(mesh):
    spec = P(("rep", "seq"), "head")
    return jax.shard_map(
        shards,
        mesh=mesh,
        in_specs=(spec, spec, spec, spec, P("rep"), P()),
        out_specs=(spec, spec, spec),
        check_vma=False,
    )
```

```python
import functools
import math

import jax
import jax.numpy as jnp
from jax import lax
from jax.experimental import pallas as pl
from jax.experimental.pallas import tpu as pltpu
from jax.sharding import PartitionSpec as P


HEADS = 32
HDIM = 128
SCALE = HDIM ** (-0.5)
LOG2_SCALE = SCALE * math.log2(math.e)
NEG = -1e30
GRAIN = 32
BLOCK = 256
F32 = jnp.float32
BF16 = jnp.bfloat16


def up(x, m):
    return (x + m - 1) // m * m


def dot_nt(a, b):
    return lax.dot_general(a, b, (((1,), (1,)), ((), ())), preferred_element_type=F32)


def dot_nn(a, b):
    return lax.dot_general(a, b, (((1,), (0,)), ((), ())), preferred_element_type=F32)


def dot_tn(a, b):
    return lax.dot_general(a, b, (((0,), (0,)), ((), ())), preferred_element_type=F32)


def query_blocks(rows):
    return [(q0, min(BLOCK, rows - q0)) for q0 in range(0, rows, BLOCK)]


def iotas(k0, kn, q0, w):
    key = k0 + lax.broadcasted_iota(jnp.int32, (kn, w), 0)
    query = q0 + lax.broadcasted_iota(jnp.int32, (1, w), 1)
    return key, query


def meta_kernel(heads, grain, caps, shift_ref, order_ref, out_ref, flag_ref):
    base = lax.axis_index("head") * heads
    for h in range(heads):
        flag_ref[h] = 0
    for i in range(HEADS // 2):
        loc = order_ref[i] - base

        @pl.when((loc >= 0) & (loc < heads))
        def _():
            flag_ref[loc] = 1

    count = flag_ref[0]
    for h in range(1, heads):
        count = count + flag_ref[h]
    yes, no = jnp.int32(0), count
    for h in range(heads):
        flag = flag_ref[h]
        out_ref[jnp.where(flag > 0, yes, no)] = h
        yes, no = yes + flag, no + 1 - flag
    off = shift_ref[0]
    slot = (off + grain - 1) // grain * grain
    pick = jnp.where(count > 0, 1, 0)
    for cap in caps[:-1]:
        pick = pick + jnp.where(count * slot > cap, 1, 0)
    out_ref[heads] = count
    out_ref[heads + 1] = off
    out_ref[heads + 2] = slot
    out_ref[heads + 3] = pick


def shifted_at(heads):
    return lambda s, m: m[jnp.minimum(s, m[heads] - 1)]


def pack_kernel(heads, base, sizes, meta, q_ref, d_ref, out_ref, sem):
    count, slot = meta[heads], meta[heads + 2]

    def each(act):
        def step(s, c):
            column = pl.multiple_of(meta[s] * HDIM, HDIM)

            def copy(at, size, i):
                src = pl.multiple_of(at, GRAIN)
                dst = pl.multiple_of(s * slot + at, GRAIN)
                for j, ref in enumerate((q_ref, d_ref)):
                    act(
                        pltpu.make_async_copy(
                            ref.at[pl.ds(src, size), pl.ds(column, HDIM)],
                            out_ref.at[pl.ds(dst, size), pl.ds(j * HDIM, HDIM)],
                            sem.at[s, j, i],
                        )
                    )

            copy(0, base, 0)
            at = jnp.int32(base)
            for i, size in enumerate(sizes):
                bit = ((slot - base) // size) % 2

                @pl.when(bit == 1)
                def _(at=at, size=size, i=i):
                    copy(at, size, i + 1)

                at = at + bit * size
            return c

        lax.fori_loop(0, count, step, 0)

    each(lambda copy: copy.start())
    each(lambda copy: copy.wait())


def stats_kernel(heads, rows, reach, meta, q_ref, k_ref, v_ref, d_ref, send_ref, own_ref):
    s = pl.program_id(0)

    @pl.when(s < meta[heads])
    def _():
        off = meta[heads + 1]
        for q0, w in query_blocks(rows):
            kn = q0 + w
            key, query = iotas(0, kn, q0, w)
            low = jnp.where(query >= off, off, 0)
            sc = dot_nt(k_ref[:kn, :], q_ref[q0:kn, :]) * LOG2_SCALE
            sc = jnp.where((key <= query) & (key >= low), sc, NEG)
            top = jnp.max(sc, axis=0, keepdims=True)
            e = jnp.exp2(sc - top)
            total = jnp.sum(e, axis=0, keepdims=True)
            dp = dot_nt(v_ref[:kn, :], d_ref[q0:kn, :])
            rd = jnp.sum(e * dp, axis=0, keepdims=True) / total
            lse = top + jnp.log2(total)
            own_ref[s, 0:1, q0:kn] = lse
            own_ref[s, 1:2, q0:kn] = rd
            if q0 < reach:
                send_ref[s, 0:1, q0:kn] = lse
                send_ref[s, 1:2, q0:kn] = rd


def plain_kernel(heads, rows, meta, q_ref, k_ref, v_ref, d_ref, dq_ref, dk_ref, dv_ref, ak_ref, av_ref):
    s = pl.program_id(0)

    @pl.when(s >= meta[heads])
    def _():
        for q0, w in query_blocks(rows):
            kn = q0 + w
            qb, db = q_ref[q0:kn, :], d_ref[q0:kn, :]
            parts = ([(0, q0, False)] if q0 else []) + [(q0, w, True)]
            scores = []
            for k0, n, diagonal in parts:
                sc = dot_nt(k_ref[k0 : k0 + n, :], qb) * LOG2_SCALE
                if diagonal:
                    key, query = iotas(k0, n, q0, w)
                    sc = jnp.where(key <= query, sc, NEG)
                scores.append(sc)
            tops = [jnp.max(sc, axis=0, keepdims=True) for sc in scores]
            top = functools.reduce(jnp.maximum, tops)
            es = [jnp.exp2(sc - top) for sc in scores]
            total = sum(jnp.sum(e, axis=0, keepdims=True) for e in es)
            dps = [dot_nt(v_ref[k0 : k0 + n, :], db) for k0, n, _ in parts]
            inv = 1.0 / total
            rd = sum(jnp.sum(e * dp, axis=0, keepdims=True) for e, dp in zip(es, dps)) * inv
            dq = None
            for (k0, n, diagonal), e, dp in zip(parts, es, dps):
                p = e * inv
                ds = (p * (dp - rd)).astype(BF16)
                gv = dot_nn(p.astype(BF16), db)
                gk = dot_nn(ds, qb)
                gq = dot_tn(ds, k_ref[k0 : k0 + n, :])
                dq = gq if dq is None else dq + gq
                if diagonal:
                    av_ref[k0 : k0 + n, :] = gv
                    ak_ref[k0 : k0 + n, :] = gk
                else:
                    av_ref[k0 : k0 + n, :] += gv
                    ak_ref[k0 : k0 + n, :] += gk
            dq_ref[q0:kn, :] = (dq * SCALE).astype(BF16)
        dk_ref[...] = (ak_ref[...] * SCALE).astype(BF16)
        dv_ref[...] = av_ref[...].astype(BF16)


def cross_kernel(
    heads, rows, first, meta, k_ref, v_ref, got_ref, st_ref, _after,
    back_ref, tot_ref, gk_ref, gv_ref, buf_ref, acc_ref,
):
    s = pl.program_id(0)
    count, off, slot = meta[heads], meta[heads + 1], meta[heads + 2]
    filled = count * slot

    @pl.when(s == 0)
    def _():
        def step(i, c):
            at = pl.multiple_of(i * GRAIN, GRAIN)
            buf_ref[pl.ds(at, GRAIN), :] = got_ref[pl.ds(at, GRAIN), :]
            return c

        lax.fori_loop(0, filled // GRAIN, step, 0)
        tail = pl.multiple_of(filled, GRAIN)
        buf_ref[pl.ds(tail, BLOCK), :] = jnp.zeros((BLOCK, 2 * HDIM), BF16)

    def block(j, k0):
        q0 = pl.multiple_of(j * BLOCK, BLOCK)
        start = pl.multiple_of(s * slot + q0, GRAIN)
        qb = buf_ref[pl.ds(start, BLOCK), :HDIM]
        db = buf_ref[pl.ds(start, BLOCK), HDIM:]
        kb, vb = k_ref[k0:, :], v_ref[k0:, :]
        key = k0 + lax.broadcasted_iota(jnp.int32, (rows - k0, BLOCK), 0)
        query = q0 + lax.broadcasted_iota(jnp.int32, (1, BLOCK), 1)
        inside = query < off
        sc = dot_nt(kb, qb) * LOG2_SCALE
        sc = jnp.where(key >= off, sc, NEG)
        top = jnp.max(sc, axis=0, keepdims=True)
        e = jnp.exp2(sc - top)
        total = jnp.sum(e, axis=0, keepdims=True)
        dp = dot_nt(vb, db)
        rd = jnp.sum(e * dp, axis=0, keepdims=True) / total
        lse = top + jnp.log2(total)
        lse1 = jnp.where(inside, st_ref[s, 0:1, pl.ds(q0, BLOCK)], 0.0)
        rd1 = jnp.where(inside, st_ref[s, 1:2, pl.ds(q0, BLOCK)], 0.0)
        high = jnp.maximum(lse, lse1)
        both = high + jnp.log2(jnp.exp2(lse - high) + jnp.exp2(lse1 - high))
        rd = jnp.exp2(lse - both) * rd + jnp.exp2(lse1 - both) * rd1
        tot_ref[s, 0:1, pl.ds(q0, BLOCK)] = both
        tot_ref[s, 1:2, pl.ds(q0, BLOCK)] = rd
        p = e * jnp.where(inside, jnp.exp2(top - both), 0.0)
        ds = (p * (dp - rd)).astype(BF16)
        gv_ref[s, k0 - first :, :] += dot_nn(p.astype(BF16), db)
        gk_ref[s, k0 - first :, :] += dot_nn(ds, qb)
        acc_ref[pl.ds(start, BLOCK), :] = (dot_tn(ds, kb) * SCALE).astype(BF16)

    @pl.when(s < count)
    def _():
        gv_ref[s] = jnp.zeros(gv_ref.shape[1:], F32)
        gk_ref[s] = jnp.zeros(gk_ref.shape[1:], F32)
        starts = (first, up(2 * first, GRAIN))
        blocks = (off + BLOCK - 1) // BLOCK
        for k0, mine in ((starts[0], off < starts[1]), (starts[1], off >= starts[1])):

            @pl.when(mine)
            def _(k0=k0):
                def step(j, c):
                    block(j, k0)
                    return c

                lax.fori_loop(0, blocks, step, 0)

    @pl.when(s == pl.num_programs(0) - 1)
    def _():
        def step(i, c):
            at = pl.multiple_of(i * GRAIN, GRAIN)
            back_ref[pl.ds(at, GRAIN), :] = acc_ref[pl.ds(at, GRAIN), :]
            return c

        lax.fori_loop(0, filled // GRAIN, step, 0)


def local_kernel(
    heads, rows, first, reach, meta, q_ref, k_ref, v_ref, d_ref, own_ref, tot_ref, gk_ref, gv_ref,
    _dq, _dk, _dv, dq_ref, dk_ref, dv_ref, part_ref, ak_ref, av_ref,
):
    s = pl.program_id(0)

    @pl.when(s < meta[heads])
    def _():
        off = meta[heads + 1]
        for q0, w in query_blocks(rows):
            kn = q0 + w
            key, query = iotas(0, kn, q0, w)
            low = jnp.where(query >= off, off, 0)
            lse = own_ref[s, 0:1, q0:kn]
            rd = own_ref[s, 1:2, q0:kn]
            if q0 < reach:
                lse = jnp.where(query < off, tot_ref[s, 0:1, q0:kn], lse)
                rd = jnp.where(query < off, tot_ref[s, 1:2, q0:kn], rd)
            qb, db = q_ref[q0:kn, :], d_ref[q0:kn, :]
            sc = dot_nt(k_ref[:kn, :], qb) * LOG2_SCALE
            p = jnp.where((key <= query) & (key >= low), jnp.exp2(sc - lse), 0.0)
            dp = dot_nt(v_ref[:kn, :], db)
            ds = (p * (dp - rd)).astype(BF16)
            gv = dot_nn(p.astype(BF16), db)
            gk = dot_nn(ds, qb)
            dq = dot_tn(ds, k_ref[:kn, :]) * SCALE
            dq_ref[q0:kn, :] = dq.astype(BF16)
            if q0 < reach:
                part_ref[s, q0:kn, :] = dq
            if q0:
                av_ref[:q0, :] += gv[:q0]
                ak_ref[:q0, :] += gk[:q0]
            av_ref[q0:kn, :] = gv[q0:]
            ak_ref[q0:kn, :] = gk[q0:]
        dk_ref[:first, :] = (ak_ref[:first, :] * SCALE).astype(BF16)
        dv_ref[:first, :] = av_ref[:first, :].astype(BF16)
        dk_ref[first:, :] = ((ak_ref[first:, :] + gk_ref[s]) * SCALE).astype(BF16)
        dv_ref[first:, :] = (av_ref[first:, :] + gv_ref[s]).astype(BF16)


def add_kernel(heads, tallest, meta, part_ref, got_ref, _dq, dq_ref, stage_ref, sem):
    slot = meta[heads + 2]

    def copy(s):
        column = pl.multiple_of(meta[s] * HDIM, HDIM)
        return pltpu.make_async_copy(
            stage_ref.at[s], dq_ref.at[pl.ds(0, tallest), pl.ds(column, HDIM)], sem.at[s]
        )

    def send(s, c):
        def both(i, c):
            at = pl.multiple_of(i * GRAIN, GRAIN)
            src = pl.multiple_of(s * slot + i * GRAIN, GRAIN)
            there = got_ref[pl.ds(src, GRAIN), :].astype(F32)
            stage_ref[s, pl.ds(at, GRAIN), :] = (part_ref[s, pl.ds(at, GRAIN), :] + there).astype(BF16)
            return c

        def here(i, c):
            at = pl.multiple_of(i * GRAIN, GRAIN)
            stage_ref[s, pl.ds(at, GRAIN), :] = part_ref[s, pl.ds(at, GRAIN), :].astype(BF16)
            return c

        lax.fori_loop(0, slot // GRAIN, both, 0)
        lax.fori_loop(slot // GRAIN, tallest // GRAIN, here, 0)
        copy(s).start()
        return c

    def wait(s, c):
        copy(s).wait()
        return c

    lax.fori_loop(0, meta[heads], send, 0)
    lax.fori_loop(0, meta[heads], wait, 0)


def cost(flops, moved):
    return pl.CostEstimate(flops=int(flops), bytes_accessed=int(moved), transcendentals=0)


def params(mebibytes):
    return pltpu.CompilerParams(vmem_limit_bytes=mebibytes * 2**20)


def shards(queries, keys, values, d_out, shift, head_order):
    rows, width = queries.shape
    heads = width // HDIM
    first, last = rows // 4, rows - rows // 4
    base = first // GRAIN * GRAIN
    tallest = up(last, GRAIN)
    reach = up(last, BLOCK)
    most = heads * tallest
    fractions = (0.25, 0.38, 0.5, 0.67, 1.0)
    caps = [up(int(most * f), GRAIN) for f in fractions]
    seq = lax.axis_size("seq")
    back = [(i, (i - 1) % seq) for i in range(seq)]
    ahead = [(i, (i + 1) % seq) for i in range(seq)]

    meta = pl.pallas_call(
        functools.partial(meta_kernel, heads, GRAIN, caps),
        out_shape=jax.ShapeDtypeStruct((heads + 4,), jnp.int32),
        in_specs=[pl.BlockSpec(memory_space=pltpu.SMEM)] * 2,
        out_specs=pl.BlockSpec(memory_space=pltpu.SMEM),
        scratch_shapes=[pltpu.SMEM((heads,), jnp.int32)],
        name="meta",
    )(shift, head_order)

    at = shifted_at(heads)
    whole = jax.ShapeDtypeStruct((rows, width), BF16)
    head_spec = pl.BlockSpec((rows, HDIM), lambda s, m: (0, at(s, m)))
    plain_at = lambda s, m: m[jnp.minimum(jnp.maximum(s, m[heads]), heads - 1)]
    plain_spec = pl.BlockSpec((rows, HDIM), lambda s, m: (0, plain_at(s, m)))
    any_spec = pl.BlockSpec(memory_space=pl.ANY)
    vmem = pl.BlockSpec(memory_space=pltpu.VMEM)
    smem = pl.BlockSpec(memory_space=pltpu.SMEM)
    tile = rows * HDIM * 2
    work = 2 * rows * rows * HDIM

    def call(kernel, in_specs, out_specs, out_shape, estimate, limit, scratch=(), aliases={}):
        return pl.pallas_call(
            kernel,
            out_shape=out_shape,
            grid_spec=pltpu.PrefetchScalarGridSpec(
                num_scalar_prefetch=1,
                grid=(heads,),
                in_specs=in_specs,
                out_specs=out_specs,
                scratch_shapes=list(scratch),
            ),
            input_output_aliases=aliases,
            cost_estimate=estimate,
            compiler_params=params(limit),
        )

    def plain(meta, queries, keys, values, d_out):
        return call(
            functools.partial(plain_kernel, heads, rows),
            [plain_spec] * 4,
            [plain_spec] * 3,
            [whole] * 3,
            cost(heads / 2 * 4 * work, heads / 2 * 7 * tile),
            16,
            [pltpu.VMEM((rows, HDIM), F32)] * 2,
        )(meta, queries, keys, values, d_out)

    def branch(cap):
        def steps(meta, queries, keys, values, d_out):
            sizes, left = [], tallest - base
            while sum(sizes) < left:
                sizes.append(GRAIN * 2 ** len(sizes))
            sent = pl.pallas_call(
                functools.partial(pack_kernel, heads, base, sizes),
                out_shape=jax.ShapeDtypeStruct((cap, 2 * HDIM), BF16),
                in_specs=[smem, any_spec, any_spec],
                out_specs=vmem,
                scratch_shapes=[pltpu.SemaphoreType.DMA((heads, 2, 1 + len(sizes)))],
                cost_estimate=cost(0, 2 * cap * HDIM * 4),
                compiler_params=params(8),
                name="pack",
            )(meta, queries, d_out)
            got = lax.ppermute(sent, "seq", back)
            st_send, st_own = call(
                functools.partial(stats_kernel, heads, rows, reach),
                [head_spec] * 4,
                [vmem, vmem],
                [
                    jax.ShapeDtypeStruct((heads, 2, reach), F32),
                    jax.ShapeDtypeStruct((heads, 2, rows), F32),
                ],
                cost(heads / 2 * 2 * work, heads / 2 * 4 * tile),
                16,
            )(meta, queries, keys, values, d_out)
            st_got = lax.ppermute(st_send, "seq", back)
            dq, dk, dv = plain(meta, queries, keys, values, d_out)
            side = jax.ShapeDtypeStruct((heads, rows - first, HDIM), F32)
            back_q, tot, gk, gv = call(
                functools.partial(cross_kernel, heads, rows, first),
                [head_spec] * 2 + [vmem, vmem, any_spec],
                [vmem] * 4,
                [
                    jax.ShapeDtypeStruct((cap, HDIM), BF16),
                    jax.ShapeDtypeStruct((heads, 2, reach), F32),
                    side,
                    side,
                ],
                cost(heads / 2 * 5 * work, heads / 2 * 6 * tile),
                24,
                [pltpu.VMEM((cap + BLOCK, 2 * HDIM), BF16), pltpu.VMEM((cap + BLOCK, HDIM), BF16)],
            )(meta, keys, values, got, st_got, dq)
            tot_got = lax.ppermute(tot, "seq", ahead)
            dq_got = lax.ppermute(back_q, "seq", ahead)
            dq, dk, dv, part = call(
                functools.partial(local_kernel, heads, rows, first, reach),
                [head_spec] * 4
                + [vmem] * 4
                + [any_spec] * 3,
                [head_spec] * 3 + [vmem],
                [whole] * 3 + [jax.ShapeDtypeStruct((heads, reach, HDIM), F32)],
                cost(heads / 2 * 4 * work, heads / 2 * 9 * tile),
                24,
                [pltpu.VMEM((rows, HDIM), F32)] * 2,
                {9: 0, 10: 1, 11: 2},
            )(meta, queries, keys, values, d_out, st_own, tot_got, gk, gv, dq, dk, dv)
            dq = pl.pallas_call(
                functools.partial(add_kernel, heads, tallest),
                out_shape=whole,
                in_specs=[smem, vmem, vmem, any_spec],
                out_specs=any_spec,
                scratch_shapes=[
                    pltpu.VMEM((heads, tallest, HDIM), BF16),
                    pltpu.SemaphoreType.DMA((heads,)),
                ],
                input_output_aliases={3: 0},
                cost_estimate=cost(0, heads / 2 * 3 * tile),
                compiler_params=params(16),
                name="add",
            )(meta, part, dq_got, dq)
            return dq, dk, dv

        return steps

    return tuple(
        lax.switch(
            meta[heads + 3],
            [plain] + [branch(cap) for cap in caps],
            meta,
            queries,
            keys,
            values,
            d_out,
        )
    )


def solution(mesh):
    spec = P(("rep", "seq"), "head")
    return jax.shard_map(
        shards,
        mesh=mesh,
        in_specs=(spec, spec, spec, spec, P("rep"), P()),
        out_specs=(spec, spec, spec),
        check_vma=False,
    )
```

```python
import functools
import math

import jax
import jax.numpy as jnp
from jax import lax
from jax.experimental import pallas as pl
from jax.experimental.pallas import tpu as pltpu
from jax.sharding import PartitionSpec as P


HEADS = 32
HDIM = 128
SCALE = HDIM ** (-0.5)
LOG2_SCALE = SCALE * math.log2(math.e)
NEG = -1e30
GRAIN = 32
BLOCK = 256
PART = 0.6
F32 = jnp.float32
BF16 = jnp.bfloat16


def up(x, m):
    return (x + m - 1) // m * m


def dot_nt(a, b):
    return lax.dot_general(a, b, (((1,), (1,)), ((), ())), preferred_element_type=F32)


def dot_nn(a, b):
    return lax.dot_general(a, b, (((1,), (0,)), ((), ())), preferred_element_type=F32)


def dot_tn(a, b):
    return lax.dot_general(a, b, (((0,), (0,)), ((), ())), preferred_element_type=F32)


def query_blocks(rows):
    return [(q0, min(BLOCK, rows - q0)) for q0 in range(0, rows, BLOCK)]


def iotas(k0, kn, q0, w):
    key = k0 + lax.broadcasted_iota(jnp.int32, (kn, w), 0)
    query = q0 + lax.broadcasted_iota(jnp.int32, (1, w), 1)
    return key, query


def meta_kernel(heads, grain, caps, shift_ref, order_ref, out_ref, flag_ref):
    base = lax.axis_index("head") * heads
    for h in range(heads):
        flag_ref[h] = 0
    for i in range(HEADS // 2):
        loc = order_ref[i] - base

        @pl.when((loc >= 0) & (loc < heads))
        def _():
            flag_ref[loc] = 1

    count = flag_ref[0]
    for h in range(1, heads):
        count = count + flag_ref[h]
    yes, no = jnp.int32(0), count
    for h in range(heads):
        flag = flag_ref[h]
        out_ref[jnp.where(flag > 0, yes, no)] = h
        yes, no = yes + flag, no + 1 - flag
    off = shift_ref[0]
    slot = (off + grain - 1) // grain * grain
    pick = jnp.where(count > 0, 1, 0)
    for cap in caps[:-1]:
        pick = pick + jnp.where(count * slot > cap, 1, 0)
    out_ref[heads] = count
    out_ref[heads + 1] = off
    out_ref[heads + 2] = slot
    out_ref[heads + 3] = pick


def shifted_at(heads):
    return lambda s, m: m[jnp.minimum(s, m[heads] - 1)]


def pack_kernel(heads, base, sizes, meta, q_ref, d_ref, one_ref, two_ref, sem, mid_ref):
    count, slot = meta[heads], meta[heads + 2]
    split = one_ref.shape[0]

    def each(act):
        def step(s, c):
            column = pl.multiple_of(meta[s] * HDIM, HDIM)
            low = s * slot
            for ref, shift, mine in (
                (one_ref, low, low + slot <= split),
                (two_ref, low - split, low >= split),
                (mid_ref, 0, (low < split) & (low + slot > split)),
            ):

                def copy(at, size, i, ref=ref, shift=shift):
                    src = pl.multiple_of(at, GRAIN)
                    dst = pl.multiple_of(shift + at, GRAIN)
                    for j, from_ref in enumerate((q_ref, d_ref)):
                        act(
                            pltpu.make_async_copy(
                                from_ref.at[pl.ds(src, size), pl.ds(column, HDIM)],
                                ref.at[pl.ds(dst, size), pl.ds(j * HDIM, HDIM)],
                                sem.at[s, j, i],
                            )
                        )

                @pl.when(mine)
                def _(copy=copy):
                    copy(0, base, 0)
                    at = jnp.int32(base)
                    for i, size in enumerate(sizes):
                        bit = ((slot - base) // size) % 2

                        @pl.when(bit == 1)
                        def _(at=at, size=size, i=i):
                            copy(at, size, i + 1)

                        at = at + bit * size

            return c

        lax.fori_loop(0, count, step, 0)

    each(lambda copy: copy.start())
    each(lambda copy: copy.wait())
    low = split // slot * slot
    cut = split - low

    @pl.when((low < count * slot) & (cut > 0))
    def _():
        def front(i, c):
            src = pl.multiple_of(i * GRAIN, GRAIN)
            dst = pl.multiple_of(low + i * GRAIN, GRAIN)
            one_ref[pl.ds(dst, GRAIN), :] = mid_ref[pl.ds(src, GRAIN), :]
            return c

        def rest(i, c):
            src = pl.multiple_of(cut + i * GRAIN, GRAIN)
            dst = pl.multiple_of(i * GRAIN, GRAIN)
            two_ref[pl.ds(dst, GRAIN), :] = mid_ref[pl.ds(src, GRAIN), :]
            return c

        lax.fori_loop(0, cut // GRAIN, front, 0)
        lax.fori_loop(0, (slot - cut) // GRAIN, rest, 0)


def stats_kernel(heads, rows, reach, meta, q_ref, k_ref, v_ref, d_ref, send_ref, own_ref):
    s = pl.program_id(0)

    @pl.when(s < meta[heads])
    def _():
        off = meta[heads + 1]
        for q0, w in query_blocks(rows):
            kn = q0 + w
            key, query = iotas(0, kn, q0, w)
            low = jnp.where(query >= off, off, 0)
            sc = dot_nt(k_ref[:kn, :], q_ref[q0:kn, :]) * LOG2_SCALE
            sc = jnp.where((key <= query) & (key >= low), sc, NEG)
            top = jnp.max(sc, axis=0, keepdims=True)
            e = jnp.exp2(sc - top)
            total = jnp.sum(e, axis=0, keepdims=True)
            dp = dot_nt(v_ref[:kn, :], d_ref[q0:kn, :])
            rd = jnp.sum(e * dp, axis=0, keepdims=True) / total
            lse = top + jnp.log2(total)
            own_ref[s, 0:1, q0:kn] = lse
            own_ref[s, 1:2, q0:kn] = rd
            if q0 < reach:
                send_ref[s, 0:1, q0:kn] = lse
                send_ref[s, 1:2, q0:kn] = rd


def plain_kernel(heads, rows, meta, q_ref, k_ref, v_ref, d_ref, dq_ref, dk_ref, dv_ref, ak_ref, av_ref):
    s = pl.program_id(0)

    @pl.when(s >= meta[heads])
    def _():
        for q0, w in query_blocks(rows):
            kn = q0 + w
            qb, db = q_ref[q0:kn, :], d_ref[q0:kn, :]
            parts = ([(0, q0, False)] if q0 else []) + [(q0, w, True)]
            scores = []
            for k0, n, diagonal in parts:
                sc = dot_nt(k_ref[k0 : k0 + n, :], qb) * LOG2_SCALE
                if diagonal:
                    key, query = iotas(k0, n, q0, w)
                    sc = jnp.where(key <= query, sc, NEG)
                scores.append(sc)
            tops = [jnp.max(sc, axis=0, keepdims=True) for sc in scores]
            top = functools.reduce(jnp.maximum, tops)
            es = [jnp.exp2(sc - top) for sc in scores]
            total = sum(jnp.sum(e, axis=0, keepdims=True) for e in es)
            dps = [dot_nt(v_ref[k0 : k0 + n, :], db) for k0, n, _ in parts]
            inv = 1.0 / total
            rd = sum(jnp.sum(e * dp, axis=0, keepdims=True) for e, dp in zip(es, dps)) * inv
            dq = None
            for (k0, n, diagonal), e, dp in zip(parts, es, dps):
                p = e * inv
                ds = (p * (dp - rd)).astype(BF16)
                gv = dot_nn(p.astype(BF16), db)
                gk = dot_nn(ds, qb)
                gq = dot_tn(ds, k_ref[k0 : k0 + n, :])
                dq = gq if dq is None else dq + gq
                if diagonal:
                    av_ref[k0 : k0 + n, :] = gv
                    ak_ref[k0 : k0 + n, :] = gk
                else:
                    av_ref[k0 : k0 + n, :] += gv
                    ak_ref[k0 : k0 + n, :] += gk
            dq_ref[q0:kn, :] = (dq * SCALE).astype(BF16)
        dk_ref[...] = (ak_ref[...] * SCALE).astype(BF16)
        dv_ref[...] = av_ref[...].astype(BF16)


def cross_kernel(heads, rows, first, split, later, meta, *refs):
    if later:
        (k_ref, v_ref, one_ref, two_ref, st_ref, back0_ref, tot0_ref, gk0_ref, gv0_ref,
         back_ref, tot_ref, gk_ref, gv_ref, buf_ref, acc_ref) = refs
    else:
        (k_ref, v_ref, one_ref, st_ref, _,
         back_ref, tot_ref, gk_ref, gv_ref, buf_ref, acc_ref) = refs
    s = pl.program_id(0)
    count, off, slot = meta[heads], meta[heads + 1], meta[heads + 2]
    done = jnp.minimum(count, split // slot)
    low, high = (done, count) if later else (0, done)

    def move(dst_ref, src_ref, start, stop, shift):
        def step(i, c):
            dst = pl.multiple_of(start + i * GRAIN, GRAIN)
            src = pl.multiple_of(start - shift + i * GRAIN, GRAIN)
            dst_ref[pl.ds(dst, GRAIN), :] = src_ref[pl.ds(src, GRAIN), :]
            return c

        lax.fori_loop(0, (stop - start) // GRAIN, step, 0)

    @pl.when((s == 0) & (low < high))
    def _():
        filled = high * slot
        if later:
            edge = jnp.minimum(filled, split)
            move(buf_ref, one_ref, low * slot, edge, 0)
            move(buf_ref, two_ref, edge, filled, split)
        else:
            move(buf_ref, one_ref, 0, filled, 0)
        tail = pl.multiple_of(filled, GRAIN)
        buf_ref[pl.ds(tail, BLOCK), :] = jnp.zeros((BLOCK, 2 * HDIM), BF16)

    def block(j, k0):
        q0 = pl.multiple_of(j * BLOCK, BLOCK)
        start = pl.multiple_of(s * slot + q0, GRAIN)
        qb = buf_ref[pl.ds(start, BLOCK), :HDIM]
        db = buf_ref[pl.ds(start, BLOCK), HDIM:]
        kb, vb = k_ref[k0:, :], v_ref[k0:, :]
        key = k0 + lax.broadcasted_iota(jnp.int32, (rows - k0, BLOCK), 0)
        query = q0 + lax.broadcasted_iota(jnp.int32, (1, BLOCK), 1)
        inside = query < off
        sc = dot_nt(kb, qb) * LOG2_SCALE
        sc = jnp.where(key >= off, sc, NEG)
        top = jnp.max(sc, axis=0, keepdims=True)
        e = jnp.exp2(sc - top)
        total = jnp.sum(e, axis=0, keepdims=True)
        dp = dot_nt(vb, db)
        rd = jnp.sum(e * dp, axis=0, keepdims=True) / total
        lse = top + jnp.log2(total)
        lse1 = jnp.where(inside, st_ref[s, 0:1, pl.ds(q0, BLOCK)], 0.0)
        rd1 = jnp.where(inside, st_ref[s, 1:2, pl.ds(q0, BLOCK)], 0.0)
        high = jnp.maximum(lse, lse1)
        both = high + jnp.log2(jnp.exp2(lse - high) + jnp.exp2(lse1 - high))
        rd = jnp.exp2(lse - both) * rd + jnp.exp2(lse1 - both) * rd1
        tot_ref[s, 0:1, pl.ds(q0, BLOCK)] = both
        tot_ref[s, 1:2, pl.ds(q0, BLOCK)] = rd
        p = e * jnp.where(inside, jnp.exp2(top - both), 0.0)
        ds = (p * (dp - rd)).astype(BF16)
        gv_ref[s, k0 - first :, :] += dot_nn(p.astype(BF16), db)
        gk_ref[s, k0 - first :, :] += dot_nn(ds, qb)
        acc_ref[pl.ds(start, BLOCK), :] = (dot_tn(ds, kb) * SCALE).astype(BF16)

    if later:

        @pl.when(s < low)
        def _():
            tot_ref[s] = tot0_ref[s]
            gk_ref[s] = gk0_ref[s]
            gv_ref[s] = gv0_ref[s]

    @pl.when((s >= low) & (s < high))
    def _():
        gv_ref[s] = jnp.zeros(gv_ref.shape[1:], F32)
        gk_ref[s] = jnp.zeros(gk_ref.shape[1:], F32)
        starts = (first, up(2 * first, GRAIN))
        blocks = (off + BLOCK - 1) // BLOCK
        for k0, mine in ((starts[0], off < starts[1]), (starts[1], off >= starts[1])):

            @pl.when(mine)
            def _(k0=k0):
                def step(j, c):
                    block(j, k0)
                    return c

                lax.fori_loop(0, blocks, step, 0)

    @pl.when(s == pl.num_programs(0) - 1)
    def _():
        if later:
            move(back_ref, back0_ref, 0, low * slot, 0)
        move(back_ref, acc_ref, low * slot, high * slot, 0)


def local_kernel(
    heads, rows, first, reach, meta, q_ref, k_ref, v_ref, d_ref, own_ref, tot_ref, gk_ref, gv_ref,
    _dq, _dk, _dv, dq_ref, dk_ref, dv_ref, part_ref, ak_ref, av_ref,
):
    s = pl.program_id(0)

    @pl.when(s < meta[heads])
    def _():
        off = meta[heads + 1]
        for q0, w in query_blocks(rows):
            kn = q0 + w
            key, query = iotas(0, kn, q0, w)
            low = jnp.where(query >= off, off, 0)
            lse = own_ref[s, 0:1, q0:kn]
            rd = own_ref[s, 1:2, q0:kn]
            if q0 < reach:
                lse = jnp.where(query < off, tot_ref[s, 0:1, q0:kn], lse)
                rd = jnp.where(query < off, tot_ref[s, 1:2, q0:kn], rd)
            qb, db = q_ref[q0:kn, :], d_ref[q0:kn, :]
            sc = dot_nt(k_ref[:kn, :], qb) * LOG2_SCALE
            p = jnp.where((key <= query) & (key >= low), jnp.exp2(sc - lse), 0.0)
            dp = dot_nt(v_ref[:kn, :], db)
            ds = (p * (dp - rd)).astype(BF16)
            gv = dot_nn(p.astype(BF16), db)
            gk = dot_nn(ds, qb)
            dq = dot_tn(ds, k_ref[:kn, :]) * SCALE
            dq_ref[q0:kn, :] = dq.astype(BF16)
            if q0 < reach:
                part_ref[s, q0:kn, :] = dq
            if q0:
                av_ref[:q0, :] += gv[:q0]
                ak_ref[:q0, :] += gk[:q0]
            av_ref[q0:kn, :] = gv[q0:]
            ak_ref[q0:kn, :] = gk[q0:]
        dk_ref[:first, :] = (ak_ref[:first, :] * SCALE).astype(BF16)
        dv_ref[:first, :] = av_ref[:first, :].astype(BF16)
        dk_ref[first:, :] = ((ak_ref[first:, :] + gk_ref[s]) * SCALE).astype(BF16)
        dv_ref[first:, :] = (av_ref[first:, :] + gv_ref[s]).astype(BF16)


def add_kernel(heads, tallest, meta, part_ref, got_ref, _dq, dq_ref, stage_ref, sem):
    slot = meta[heads + 2]

    def copy(s):
        column = pl.multiple_of(meta[s] * HDIM, HDIM)
        return pltpu.make_async_copy(
            stage_ref.at[s], dq_ref.at[pl.ds(0, tallest), pl.ds(column, HDIM)], sem.at[s]
        )

    def send(s, c):
        def both(i, c):
            at = pl.multiple_of(i * GRAIN, GRAIN)
            src = pl.multiple_of(s * slot + i * GRAIN, GRAIN)
            there = got_ref[pl.ds(src, GRAIN), :].astype(F32)
            stage_ref[s, pl.ds(at, GRAIN), :] = (part_ref[s, pl.ds(at, GRAIN), :] + there).astype(BF16)
            return c

        def here(i, c):
            at = pl.multiple_of(i * GRAIN, GRAIN)
            stage_ref[s, pl.ds(at, GRAIN), :] = part_ref[s, pl.ds(at, GRAIN), :].astype(BF16)
            return c

        lax.fori_loop(0, slot // GRAIN, both, 0)
        lax.fori_loop(slot // GRAIN, tallest // GRAIN, here, 0)
        copy(s).start()
        return c

    def wait(s, c):
        copy(s).wait()
        return c

    lax.fori_loop(0, meta[heads], send, 0)
    lax.fori_loop(0, meta[heads], wait, 0)


def cost(flops, moved):
    return pl.CostEstimate(flops=int(flops), bytes_accessed=int(moved), transcendentals=0)


def params(mebibytes):
    return pltpu.CompilerParams(vmem_limit_bytes=mebibytes * 2**20)


def shards(queries, keys, values, d_out, shift, head_order):
    rows, width = queries.shape
    heads = width // HDIM
    first, last = rows // 4, rows - rows // 4
    base = first // GRAIN * GRAIN
    tallest = up(last, GRAIN)
    reach = up(last, BLOCK)
    most = heads * tallest
    fractions = (0.36, 0.52, 0.7, 1.0)
    caps = [up(int(most * f), GRAIN) for f in fractions]
    seq = lax.axis_size("seq")
    back = [(i, (i - 1) % seq) for i in range(seq)]
    ahead = [(i, (i + 1) % seq) for i in range(seq)]

    meta = pl.pallas_call(
        functools.partial(meta_kernel, heads, GRAIN, caps),
        out_shape=jax.ShapeDtypeStruct((heads + 4,), jnp.int32),
        in_specs=[pl.BlockSpec(memory_space=pltpu.SMEM)] * 2,
        out_specs=pl.BlockSpec(memory_space=pltpu.SMEM),
        scratch_shapes=[pltpu.SMEM((heads,), jnp.int32)],
        name="meta",
    )(shift, head_order)

    at = shifted_at(heads)
    whole = jax.ShapeDtypeStruct((rows, width), BF16)
    head_spec = pl.BlockSpec((rows, HDIM), lambda s, m: (0, at(s, m)))
    plain_at = lambda s, m: m[jnp.minimum(jnp.maximum(s, m[heads]), heads - 1)]
    plain_spec = pl.BlockSpec((rows, HDIM), lambda s, m: (0, plain_at(s, m)))
    any_spec = pl.BlockSpec(memory_space=pl.ANY)
    vmem = pl.BlockSpec(memory_space=pltpu.VMEM)
    smem = pl.BlockSpec(memory_space=pltpu.SMEM)
    tile = rows * HDIM * 2
    work = 2 * rows * rows * HDIM

    def call(kernel, in_specs, out_specs, out_shape, estimate, limit, scratch=(), aliases={}):
        return pl.pallas_call(
            kernel,
            out_shape=out_shape,
            grid_spec=pltpu.PrefetchScalarGridSpec(
                num_scalar_prefetch=1,
                grid=(heads,),
                in_specs=in_specs,
                out_specs=out_specs,
                scratch_shapes=list(scratch),
            ),
            input_output_aliases=aliases,
            cost_estimate=estimate,
            compiler_params=params(limit),
        )

    def plain(meta, queries, keys, values, d_out):
        return call(
            functools.partial(plain_kernel, heads, rows),
            [plain_spec] * 4,
            [plain_spec] * 3,
            [whole] * 3,
            cost(heads / 2 * 4 * work, heads / 2 * 7 * tile),
            16,
            [pltpu.VMEM((rows, HDIM), F32)] * 2,
        )(meta, queries, keys, values, d_out)

    def branch(cap):
        def steps(meta, queries, keys, values, d_out):
            sizes, left = [], tallest - base
            while sum(sizes) < left:
                sizes.append(GRAIN * 2 ** len(sizes))
            split = up(int(cap * PART), GRAIN)
            shapes = [jax.ShapeDtypeStruct((n, 2 * HDIM), BF16) for n in (split, cap - split)]
            one, two = pl.pallas_call(
                functools.partial(pack_kernel, heads, base, sizes),
                out_shape=shapes,
                in_specs=[smem, any_spec, any_spec],
                out_specs=[vmem, vmem],
                scratch_shapes=[
                    pltpu.SemaphoreType.DMA((heads, 2, 1 + len(sizes))),
                    pltpu.VMEM((tallest, 2 * HDIM), BF16),
                ],
                cost_estimate=cost(0, 2 * cap * HDIM * 4),
                compiler_params=params(8),
                name="pack",
            )(meta, queries, d_out)
            one_got = lax.ppermute(one, "seq", back)
            st_send, st_own = call(
                functools.partial(stats_kernel, heads, rows, reach),
                [head_spec] * 4,
                [vmem, vmem],
                [
                    jax.ShapeDtypeStruct((heads, 2, reach), F32),
                    jax.ShapeDtypeStruct((heads, 2, rows), F32),
                ],
                cost(heads / 2 * 2 * work, heads / 2 * 4 * tile),
                16,
            )(meta, queries, keys, values, d_out)
            st_got = lax.ppermute(st_send, "seq", back)
            two_got = lax.ppermute(two, "seq", back)
            dq, dk, dv = plain(meta, queries, keys, values, d_out)
            side = jax.ShapeDtypeStruct((heads, rows - first, HDIM), F32)

            def cross(later, size, *args):
                def block_of(s, m):
                    done = jnp.minimum(m[heads], split // m[heads + 2])
                    low, high = (done, m[heads]) if later else (0, done)
                    s = jnp.maximum(jnp.minimum(s, high - 1), low)
                    return (0, m[jnp.minimum(s, heads - 1)])

                mine = pl.BlockSpec((rows, HDIM), block_of)
                return call(
                    functools.partial(cross_kernel, heads, rows, first, split, later),
                    [mine] * 2 + ([vmem] * 7 if later else [vmem, vmem, any_spec]),
                    [vmem] * 4,
                    [
                        jax.ShapeDtypeStruct((size, HDIM), BF16),
                        jax.ShapeDtypeStruct((heads, 2, reach), F32),
                        side,
                        side,
                    ],
                    cost(heads / 4 * 5 * work, heads / 4 * 6 * tile),
                    20,
                    [
                        pltpu.VMEM((size + BLOCK, 2 * HDIM), BF16),
                        pltpu.VMEM((size + BLOCK, HDIM), BF16),
                    ],
                )(meta, keys, values, *args)

            begun = cross(False, split, one_got, st_got, dq)
            back_q, tot, gk, gv = cross(True, cap, one_got, two_got, st_got, *begun)
            tot_got = lax.ppermute(tot, "seq", ahead)
            dq_got = lax.ppermute(back_q, "seq", ahead)
            dq, dk, dv, part = call(
                functools.partial(local_kernel, heads, rows, first, reach),
                [head_spec] * 4
                + [vmem] * 4
                + [any_spec] * 3,
                [head_spec] * 3 + [vmem],
                [whole] * 3 + [jax.ShapeDtypeStruct((heads, reach, HDIM), F32)],
                cost(heads / 2 * 4 * work, heads / 2 * 9 * tile),
                24,
                [pltpu.VMEM((rows, HDIM), F32)] * 2,
                {9: 0, 10: 1, 11: 2},
            )(meta, queries, keys, values, d_out, st_own, tot_got, gk, gv, dq, dk, dv)
            dq = pl.pallas_call(
                functools.partial(add_kernel, heads, tallest),
                out_shape=whole,
                in_specs=[smem, vmem, vmem, any_spec],
                out_specs=any_spec,
                scratch_shapes=[
                    pltpu.VMEM((heads, tallest, HDIM), BF16),
                    pltpu.SemaphoreType.DMA((heads,)),
                ],
                input_output_aliases={3: 0},
                cost_estimate=cost(0, heads / 2 * 3 * tile),
                compiler_params=params(16),
                name="add",
            )(meta, part, dq_got, dq)
            return dq, dk, dv

        return steps

    return tuple(
        lax.switch(
            meta[heads + 3],
            [plain] + [branch(cap) for cap in caps],
            meta,
            queries,
            keys,
            values,
            d_out,
        )
    )


def solution(mesh):
    spec = P(("rep", "seq"), "head")
    return jax.shard_map(
        shards,
        mesh=mesh,
        in_specs=(spec, spec, spec, spec, P("rep"), P()),
        out_specs=(spec, spec, spec),
        check_vma=False,
    )
```

```python
import functools
import math

import jax
import jax.numpy as jnp
from jax import lax
from jax.experimental import pallas as pl
from jax.experimental.pallas import tpu as pltpu
from jax.sharding import PartitionSpec as P


HEADS = 32
HDIM = 128
SCALE = HDIM ** (-0.5)
LOG2_SCALE = SCALE * math.log2(math.e)
NEG = -1e30
GRAIN = 32
BLOCK = 256
PART = 0.6
F32 = jnp.float32
BF16 = jnp.bfloat16


def up(x, m):
    return (x + m - 1) // m * m


def dot_nt(a, b):
    return lax.dot_general(a, b, (((1,), (1,)), ((), ())), preferred_element_type=F32)


def dot_nn(a, b):
    return lax.dot_general(a, b, (((1,), (0,)), ((), ())), preferred_element_type=F32)


def dot_tn(a, b):
    return lax.dot_general(a, b, (((0,), (0,)), ((), ())), preferred_element_type=F32)


def query_blocks(rows):
    return [(q0, min(BLOCK, rows - q0)) for q0 in range(0, rows, BLOCK)]


def mask_of(q0, w, diagonal, low=None):
    k0, kn = (q0, w) if diagonal else (0, q0)
    key = k0 + lax.broadcasted_iota(jnp.int32, (kn, w), 0)
    query = q0 + lax.broadcasted_iota(jnp.int32, (1, w), 1)
    if low is None:
        return key <= query
    return (key >= low) & (key <= query) if diagonal else key >= low


def masked(x, q0, w, other, low=None):
    below = jnp.where(mask_of(q0, w, True, low), x[q0:], other)
    if not q0:
        return below
    above = x[:q0] if low is None else jnp.where(mask_of(q0, w, False, low), x[:q0], other)
    return jnp.concatenate([above, below], axis=0)


def staggered(blocks, front, back):
    held = None
    for block in blocks:
        fresh = front(*block)
        if held is not None:
            back(*held)
        held = (*block, fresh)
    back(*held)


def column(meta, s):
    return pl.ds(pl.multiple_of(meta[s] * HDIM, HDIM), HDIM)


def written_out(start, stop, copies, compute):
    def finish(s):
        for copy in copies(s):
            copy.wait()

    def step(s, c):
        @pl.when(s >= start + 2)
        def _():
            finish(s - 2)

        compute(s)
        for copy in copies(s):
            copy.start()
        return c

    lax.fori_loop(start, stop, step, 0)
    for back in (2, 1):

        @pl.when(stop - back >= start)
        def _(back=back):
            finish(stop - back)


def meta_kernel(heads, grain, caps, shift_ref, order_ref, out_ref, flag_ref):
    base = lax.axis_index("head") * heads
    for h in range(heads):
        flag_ref[h] = 0
    for i in range(HEADS // 2):
        loc = order_ref[i] - base

        @pl.when((loc >= 0) & (loc < heads))
        def _():
            flag_ref[loc] = 1

    count = flag_ref[0]
    for h in range(1, heads):
        count = count + flag_ref[h]
    yes, no = jnp.int32(0), count
    for h in range(heads):
        flag = flag_ref[h]
        out_ref[jnp.where(flag > 0, yes, no)] = h
        yes, no = yes + flag, no + 1 - flag
    off = shift_ref[0]
    slot = (off + grain - 1) // grain * grain
    pick = jnp.where(count > 0, 1, 0)
    for cap in caps[:-1]:
        pick = pick + jnp.where(count * slot > cap, 1, 0)
    out_ref[heads] = count
    out_ref[heads + 1] = off
    out_ref[heads + 2] = slot
    out_ref[heads + 3] = pick


def pack_kernel(heads, base, sizes, meta, q_ref, d_ref, one_ref, two_ref, sem, mid_ref):
    count, slot = meta[heads], meta[heads + 2]
    split = one_ref.shape[0]

    def each(act):
        def step(s, c):
            column = pl.multiple_of(meta[s] * HDIM, HDIM)
            low = s * slot
            for ref, shift, mine in (
                (one_ref, low, low + slot <= split),
                (two_ref, low - split, low >= split),
                (mid_ref, 0, (low < split) & (low + slot > split)),
            ):

                def copy(at, size, i, ref=ref, shift=shift):
                    src = pl.multiple_of(at, GRAIN)
                    dst = pl.multiple_of(shift + at, GRAIN)
                    for j, from_ref in enumerate((q_ref, d_ref)):
                        act(
                            pltpu.make_async_copy(
                                from_ref.at[pl.ds(src, size), pl.ds(column, HDIM)],
                                ref.at[pl.ds(dst, size), pl.ds(j * HDIM, HDIM)],
                                sem.at[s, j, i],
                            )
                        )

                @pl.when(mine)
                def _(copy=copy):
                    copy(0, base, 0)
                    at = jnp.int32(base)
                    for i, size in enumerate(sizes):
                        bit = ((slot - base) // size) % 2

                        @pl.when(bit == 1)
                        def _(at=at, size=size, i=i):
                            copy(at, size, i + 1)

                        at = at + bit * size

            return c

        lax.fori_loop(0, count, step, 0)

    each(lambda copy: copy.start())
    each(lambda copy: copy.wait())
    low = split // slot * slot
    cut = split - low

    @pl.when((low < count * slot) & (cut > 0))
    def _():
        def front(i, c):
            src = pl.multiple_of(i * GRAIN, GRAIN)
            dst = pl.multiple_of(low + i * GRAIN, GRAIN)
            one_ref[pl.ds(dst, GRAIN), :] = mid_ref[pl.ds(src, GRAIN), :]
            return c

        def rest(i, c):
            src = pl.multiple_of(cut + i * GRAIN, GRAIN)
            dst = pl.multiple_of(i * GRAIN, GRAIN)
            two_ref[pl.ds(dst, GRAIN), :] = mid_ref[pl.ds(src, GRAIN), :]
            return c

        lax.fori_loop(0, cut // GRAIN, front, 0)
        lax.fori_loop(0, (slot - cut) // GRAIN, rest, 0)


def stats_kernel(heads, rows, reach, meta, q_ref, k_ref, v_ref, d_ref, send_ref, own_ref):
    off = meta[heads + 1]

    def step(s, c):
        col = column(meta, s)

        def front(q0, w):
            kn = q0 + w
            sc = dot_nt(k_ref[:kn, col], q_ref[q0:kn, col]) * LOG2_SCALE
            return sc, dot_nt(v_ref[:kn, col], d_ref[q0:kn, col])

        def back(q0, w, held):
            sc, dp = held
            kn = q0 + w
            query = q0 + lax.broadcasted_iota(jnp.int32, (1, w), 1)
            sc = masked(sc, q0, w, NEG, jnp.where(query >= off, off, 0))
            top = jnp.max(sc, axis=0, keepdims=True)
            e = jnp.exp2(sc - top)
            total = jnp.sum(e, axis=0, keepdims=True)
            rd = jnp.sum(e * dp, axis=0, keepdims=True) / total
            lse = top + jnp.log2(total)
            own_ref[s, 0:1, q0:kn] = lse
            own_ref[s, 1:2, q0:kn] = rd
            if q0 < reach:
                send_ref[s, 0:1, q0:kn] = lse
                send_ref[s, 1:2, q0:kn] = rd

        staggered(query_blocks(rows), front, back)
        return c

    lax.fori_loop(0, meta[heads], step, 0)


def plain_kernel(
    heads, rows, meta, q_ref, k_ref, v_ref, d_ref, dq_ref, dk_ref, dv_ref,
    oq_ref, ok_ref, ov_ref, ak_ref, av_ref, sem,
):
    def copies(s):
        return [
            pltpu.make_async_copy(stage.at[s % 2], out.at[:, column(meta, s)], sem.at[s % 2, i])
            for i, (stage, out) in enumerate(((oq_ref, dq_ref), (ok_ref, dk_ref), (ov_ref, dv_ref)))
        ]

    def compute(s):
        col = column(meta, s)

        def front(q0, w):
            kn = q0 + w
            sc = dot_nt(k_ref[:kn, col], q_ref[q0:kn, col]) * LOG2_SCALE
            sc = masked(sc, q0, w, NEG)
            dp = dot_nt(v_ref[:kn, col], d_ref[q0:kn, col])
            top = jnp.max(sc, axis=0, keepdims=True)
            e = jnp.exp2(sc - top)
            inv = 1.0 / jnp.sum(e, axis=0, keepdims=True)
            rd = jnp.sum(e * dp, axis=0, keepdims=True) * inv
            p = e * inv
            return p.astype(BF16), (p * (dp - rd)).astype(BF16)

        def back(q0, w, held):
            accumulate(q0, w, held, col)

        def accumulate(q0, w, held, col):
            p, ds = held
            kn = q0 + w
            gv = dot_nn(p, d_ref[q0:kn, col])
            gk = dot_nn(ds, q_ref[q0:kn, col])
            oq_ref[s % 2, q0:kn, :] = (dot_tn(ds, k_ref[:kn, col]) * SCALE).astype(BF16)
            if q0:
                av_ref[:q0, :] += gv[:q0]
                ak_ref[:q0, :] += gk[:q0]
            av_ref[q0:kn, :] = gv[q0:]
            ak_ref[q0:kn, :] = gk[q0:]

        staggered(query_blocks(rows), front, back)
        ok_ref[s % 2] = (ak_ref[...] * SCALE).astype(BF16)
        ov_ref[s % 2] = av_ref[...].astype(BF16)

    written_out(meta[heads], heads, copies, compute)


def cross_kernel(heads, rows, first, reach, split, later, meta, *refs):
    if later:
        (k_ref, v_ref, one_ref, two_ref, st_ref, back0_ref, tot0_ref, gk0_ref, gv0_ref,
         back_ref, tot_ref, gk_ref, gv_ref, buf_ref, acc_ref) = refs
    else:
        (k_ref, v_ref, one_ref, st_ref, _,
         back_ref, tot_ref, gk_ref, gv_ref, buf_ref, acc_ref) = refs
    count, off, slot = meta[heads], meta[heads + 1], meta[heads + 2]
    done = jnp.minimum(count, split // slot)
    low, high = (done, count) if later else (0, done)

    def move(dst_ref, src_ref, start, stop, shift):
        def step(i, c):
            dst = pl.multiple_of(start + i * GRAIN, GRAIN)
            src = pl.multiple_of(start - shift + i * GRAIN, GRAIN)
            dst_ref[pl.ds(dst, GRAIN), :] = src_ref[pl.ds(src, GRAIN), :]
            return c

        lax.fori_loop(0, (stop - start) // GRAIN, step, 0)

    @pl.when(low < high)
    def _():
        filled = high * slot
        if later:
            edge = jnp.minimum(filled, split)
            move(buf_ref, one_ref, low * slot, edge, 0)
            move(buf_ref, two_ref, edge, filled, split)
        else:
            move(buf_ref, one_ref, 0, filled, 0)
        tail = pl.multiple_of(filled, GRAIN)
        buf_ref[pl.ds(tail, BLOCK), :] = jnp.zeros((BLOCK, 2 * HDIM), BF16)

    def one_head(s, k0, blocks):
        col = column(meta, s)

        def rows_of(q0):
            return pl.ds(pl.multiple_of(s * slot + q0, GRAIN), BLOCK)

        def front(q0):
            qb, db = buf_ref[rows_of(q0), :HDIM], buf_ref[rows_of(q0), HDIM:]
            lanes = slice(q0, q0 + BLOCK)
            key = k0 + lax.broadcasted_iota(jnp.int32, (rows - k0, BLOCK), 0)
            inside = q0 + lax.broadcasted_iota(jnp.int32, (1, BLOCK), 1) < off
            sc = dot_nt(k_ref[k0:, col], qb) * LOG2_SCALE
            sc = jnp.where(key >= off, sc, NEG)
            dp = dot_nt(v_ref[k0:, col], db)
            top = jnp.max(sc, axis=0, keepdims=True)
            e = jnp.exp2(sc - top)
            total = jnp.sum(e, axis=0, keepdims=True)
            rd = jnp.sum(e * dp, axis=0, keepdims=True) / total
            lse = top + jnp.log2(total)
            lse1 = jnp.where(inside, st_ref[s, 0:1, lanes], 0.0)
            rd1 = jnp.where(inside, st_ref[s, 1:2, lanes], 0.0)
            most = jnp.maximum(lse, lse1)
            both = most + jnp.log2(jnp.exp2(lse - most) + jnp.exp2(lse1 - most))
            rd = jnp.exp2(lse - both) * rd + jnp.exp2(lse1 - both) * rd1
            tot_ref[s, 0:1, lanes] = both
            tot_ref[s, 1:2, lanes] = rd
            p = e * jnp.where(inside, jnp.exp2(top - both), 0.0)
            return p.astype(BF16), (p * (dp - rd)).astype(BF16)

        def back(q0, held):
            p, ds = held
            qb, db = buf_ref[rows_of(q0), :HDIM], buf_ref[rows_of(q0), HDIM:]
            gv, gk = dot_nn(p, db), dot_nn(ds, qb)
            if q0:
                gv_ref[s, k0 - first :, :] += gv
                gk_ref[s, k0 - first :, :] += gk
            else:
                gv_ref[s, k0 - first :, :] = gv
                gk_ref[s, k0 - first :, :] = gk
                if k0 > first:
                    gv_ref[s, : k0 - first, :] = jnp.zeros((k0 - first, HDIM), F32)
                    gk_ref[s, : k0 - first, :] = jnp.zeros((k0 - first, HDIM), F32)
            acc_ref[rows_of(q0), :] = (dot_tn(ds, k_ref[k0:, col]) * SCALE).astype(BF16)

        staggered([(q0,) for q0 in range(0, blocks * BLOCK, BLOCK)], front, back)

    if later:

        def forward(s, c):
            tot_ref[s] = tot0_ref[s]
            gk_ref[s] = gk0_ref[s]
            gv_ref[s] = gv0_ref[s]
            return c

        lax.fori_loop(0, low, forward, 0)

    def step(s, c):
        for blocks in range(1, reach // BLOCK + 1):
            below = (blocks - 1) * BLOCK

            @pl.when((off > below) & (off <= below + BLOCK))
            def _(blocks=blocks, below=below):
                one_head(s, max(first, below), blocks)

        return c

    lax.fori_loop(low, high, step, 0)
    if later:
        move(back_ref, back0_ref, 0, low * slot, 0)
    move(back_ref, acc_ref, low * slot, high * slot, 0)


def local_kernel(
    heads, rows, first, reach, tallest, meta, q_ref, k_ref, v_ref, d_ref, own_ref, tot_ref, gk_ref, gv_ref,
    _dq, _dk, _dv, dq_ref, dk_ref, dv_ref, part_ref, oq_ref, ok_ref, ov_ref, ak_ref, av_ref, sem,
):
    off = meta[heads + 1]

    def copies(s):
        col = column(meta, s)
        return [
            pltpu.make_async_copy(
                oq_ref.at[s % 2], dq_ref.at[pl.ds(tallest, rows - tallest), col], sem.at[s % 2, 0]
            ),
            pltpu.make_async_copy(ok_ref.at[s % 2], dk_ref.at[:, col], sem.at[s % 2, 1]),
            pltpu.make_async_copy(ov_ref.at[s % 2], dv_ref.at[:, col], sem.at[s % 2, 2]),
        ]

    def compute(s):
        col = column(meta, s)

        def front(q0, w):
            kn = q0 + w
            query = q0 + lax.broadcasted_iota(jnp.int32, (1, w), 1)
            lse, rd = own_ref[s, 0:1, q0:kn], own_ref[s, 1:2, q0:kn]
            if q0 < reach:
                lse = jnp.where(query < off, tot_ref[s, 0:1, q0:kn], lse)
                rd = jnp.where(query < off, tot_ref[s, 1:2, q0:kn], rd)
            sc = dot_nt(k_ref[:kn, col], q_ref[q0:kn, col]) * LOG2_SCALE
            p = masked(jnp.exp2(sc - lse), q0, w, 0.0, jnp.where(query >= off, off, 0))
            dp = dot_nt(v_ref[:kn, col], d_ref[q0:kn, col])
            return p.astype(BF16), (p * (dp - rd)).astype(BF16)

        def back(q0, w, held):
            p, ds = held
            kn = q0 + w
            gv = dot_nn(p, d_ref[q0:kn, col])
            gk = dot_nn(ds, q_ref[q0:kn, col])
            dq = dot_tn(ds, k_ref[:kn, col]) * SCALE
            if q0 < reach:
                part_ref[s, q0:kn, :] = dq
            at = max(q0, tallest)
            if at < kn:
                oq_ref[s % 2, at - tallest : kn - tallest, :] = dq[at - q0 :].astype(BF16)
            if q0:
                av_ref[:q0, :] += gv[:q0]
                ak_ref[:q0, :] += gk[:q0]
            av_ref[q0:kn, :] = gv[q0:]
            ak_ref[q0:kn, :] = gk[q0:]

        staggered(query_blocks(rows), front, back)
        ok_ref[s % 2, :first, :] = (ak_ref[:first, :] * SCALE).astype(BF16)
        ov_ref[s % 2, :first, :] = av_ref[:first, :].astype(BF16)
        ok_ref[s % 2, first:, :] = ((ak_ref[first:, :] + gk_ref[s]) * SCALE).astype(BF16)
        ov_ref[s % 2, first:, :] = (av_ref[first:, :] + gv_ref[s]).astype(BF16)

    written_out(0, meta[heads], copies, compute)


def add_kernel(heads, tallest, meta, part_ref, got_ref, _dq, dq_ref, stage_ref, sem):
    slot = meta[heads + 2]

    def copy(s):
        column = pl.multiple_of(meta[s] * HDIM, HDIM)
        return pltpu.make_async_copy(
            stage_ref.at[s], dq_ref.at[pl.ds(0, tallest), pl.ds(column, HDIM)], sem.at[s]
        )

    def send(s, c):
        def both(i, c):
            at = pl.multiple_of(i * GRAIN, GRAIN)
            src = pl.multiple_of(s * slot + i * GRAIN, GRAIN)
            there = got_ref[pl.ds(src, GRAIN), :].astype(F32)
            stage_ref[s, pl.ds(at, GRAIN), :] = (part_ref[s, pl.ds(at, GRAIN), :] + there).astype(BF16)
            return c

        def here(i, c):
            at = pl.multiple_of(i * GRAIN, GRAIN)
            stage_ref[s, pl.ds(at, GRAIN), :] = part_ref[s, pl.ds(at, GRAIN), :].astype(BF16)
            return c

        lax.fori_loop(0, slot // GRAIN, both, 0)
        lax.fori_loop(slot // GRAIN, tallest // GRAIN, here, 0)
        copy(s).start()
        return c

    def wait(s, c):
        copy(s).wait()
        return c

    lax.fori_loop(0, meta[heads], send, 0)
    lax.fori_loop(0, meta[heads], wait, 0)


def cost(flops, moved):
    return pl.CostEstimate(flops=int(flops), bytes_accessed=int(moved), transcendentals=0)


def params(mebibytes):
    return pltpu.CompilerParams(vmem_limit_bytes=mebibytes * 2**20)


def shards(queries, keys, values, d_out, shift, head_order):
    rows, width = queries.shape
    heads = width // HDIM
    first, last = rows // 4, rows - rows // 4
    base = first // GRAIN * GRAIN
    tallest = up(last, GRAIN)
    reach = up(last, BLOCK)
    most = heads * tallest
    fractions = (0.36, 0.52, 0.7, 1.0)
    caps = [up(int(most * f), GRAIN) for f in fractions]
    seq = lax.axis_size("seq")
    back = [(i, (i - 1) % seq) for i in range(seq)]
    ahead = [(i, (i + 1) % seq) for i in range(seq)]

    meta = pl.pallas_call(
        functools.partial(meta_kernel, heads, GRAIN, caps),
        out_shape=jax.ShapeDtypeStruct((heads + 4,), jnp.int32),
        in_specs=[pl.BlockSpec(memory_space=pltpu.SMEM)] * 2,
        out_specs=pl.BlockSpec(memory_space=pltpu.SMEM),
        scratch_shapes=[pltpu.SMEM((heads,), jnp.int32)],
        name="meta",
    )(shift, head_order)

    whole = jax.ShapeDtypeStruct((rows, width), BF16)
    any_spec = pl.BlockSpec(memory_space=pl.ANY)
    vmem = pl.BlockSpec(memory_space=pltpu.VMEM)
    smem = pl.BlockSpec(memory_space=pltpu.SMEM)
    tile = rows * HDIM * 2
    work = 2 * rows * rows * HDIM

    def stages(top):
        stage = [pltpu.VMEM((2, n, HDIM), BF16) for n in (rows - top, rows, rows)]
        sums = [pltpu.VMEM((rows, HDIM), F32)] * 2
        return stage + sums + [pltpu.SemaphoreType.DMA((2, 3))]

    def call(kernel, in_specs, out_specs, out_shape, estimate, limit, scratch=(), aliases={}):
        return pl.pallas_call(
            kernel,
            out_shape=out_shape,
            in_specs=[smem] + in_specs,
            out_specs=out_specs,
            scratch_shapes=list(scratch),
            input_output_aliases=aliases,
            cost_estimate=estimate,
            compiler_params=params(limit),
        )

    def plain(meta, queries, keys, values, d_out):
        return call(
            functools.partial(plain_kernel, heads, rows),
            [vmem] * 4,
            [any_spec] * 3,
            [whole] * 3,
            cost(heads / 2 * 4 * work, heads / 2 * 7 * tile),
            16,
            stages(0),
        )(meta, queries, keys, values, d_out)

    def branch(cap):
        def steps(meta, queries, keys, values, d_out):
            sizes, left = [], tallest - base
            while sum(sizes) < left:
                sizes.append(GRAIN * 2 ** len(sizes))
            split = up(int(cap * PART), GRAIN)
            shapes = [jax.ShapeDtypeStruct((n, 2 * HDIM), BF16) for n in (split, cap - split)]
            one, two = pl.pallas_call(
                functools.partial(pack_kernel, heads, base, sizes),
                out_shape=shapes,
                in_specs=[smem, any_spec, any_spec],
                out_specs=[vmem, vmem],
                scratch_shapes=[
                    pltpu.SemaphoreType.DMA((heads, 2, 1 + len(sizes))),
                    pltpu.VMEM((tallest, 2 * HDIM), BF16),
                ],
                cost_estimate=cost(0, 2 * cap * HDIM * 4),
                compiler_params=params(8),
                name="pack",
            )(meta, queries, d_out)
            one_got = lax.ppermute(one, "seq", back)
            st_send, st_own = call(
                functools.partial(stats_kernel, heads, rows, reach),
                [vmem] * 4,
                [vmem, vmem],
                [
                    jax.ShapeDtypeStruct((heads, 2, reach), F32),
                    jax.ShapeDtypeStruct((heads, 2, rows), F32),
                ],
                cost(heads / 2 * 2 * work, heads / 2 * 4 * tile),
                16,
            )(meta, queries, keys, values, d_out)
            st_got = lax.ppermute(st_send, "seq", back)
            two_got = lax.ppermute(two, "seq", back)
            dq, dk, dv = plain(meta, queries, keys, values, d_out)
            side = jax.ShapeDtypeStruct((heads, rows - first, HDIM), F32)

            def cross(later, size, *args):
                return call(
                    functools.partial(cross_kernel, heads, rows, first, reach, split, later),
                    [vmem] * 9 if later else [vmem] * 4 + [any_spec],
                    [vmem] * 4,
                    [
                        jax.ShapeDtypeStruct((size, HDIM), BF16),
                        jax.ShapeDtypeStruct((heads, 2, reach), F32),
                        side,
                        side,
                    ],
                    cost(heads / 4 * 5 * work, heads / 4 * 6 * tile),
                    20,
                    [
                        pltpu.VMEM((size + BLOCK, 2 * HDIM), BF16),
                        pltpu.VMEM((size + BLOCK, HDIM), BF16),
                    ],
                )(meta, keys, values, *args)

            begun = cross(False, split, one_got, st_got, dq)
            back_q, tot, gk, gv = cross(True, cap, one_got, two_got, st_got, *begun)
            tot_got = lax.ppermute(tot, "seq", ahead)
            dq_got = lax.ppermute(back_q, "seq", ahead)
            dq, dk, dv, part = call(
                functools.partial(local_kernel, heads, rows, first, reach, tallest),
                [vmem] * 8 + [any_spec] * 3,
                [any_spec] * 3 + [vmem],
                [whole] * 3 + [jax.ShapeDtypeStruct((heads, reach, HDIM), F32)],
                cost(heads / 2 * 4 * work, heads / 2 * 9 * tile),
                24,
                stages(tallest),
                {9: 0, 10: 1, 11: 2},
            )(meta, queries, keys, values, d_out, st_own, tot_got, gk, gv, dq, dk, dv)
            dq = pl.pallas_call(
                functools.partial(add_kernel, heads, tallest),
                out_shape=whole,
                in_specs=[smem, vmem, vmem, any_spec],
                out_specs=any_spec,
                scratch_shapes=[
                    pltpu.VMEM((heads, tallest, HDIM), BF16),
                    pltpu.SemaphoreType.DMA((heads,)),
                ],
                input_output_aliases={3: 0},
                cost_estimate=cost(0, heads / 2 * 3 * tile),
                compiler_params=params(16),
                name="add",
            )(meta, part, dq_got, dq)
            return dq, dk, dv

        return steps

    return tuple(
        lax.switch(
            meta[heads + 3],
            [plain] + [branch(cap) for cap in caps],
            meta,
            queries,
            keys,
            values,
            d_out,
        )
    )


def solution(mesh):
    spec = P(("rep", "seq"), "head")
    return jax.shard_map(
        shards,
        mesh=mesh,
        in_specs=(spec, spec, spec, spec, P("rep"), P()),
        out_specs=(spec, spec, spec),
        check_vma=False,
    )
```

```python
import functools
import math

import jax
import jax.numpy as jnp
from jax import lax
from jax.experimental import pallas as pl
from jax.experimental.pallas import tpu as pltpu
from jax.sharding import PartitionSpec as P


HEADS = 32
HDIM = 128
SCALE = HDIM ** (-0.5)
LOG2_SCALE = SCALE * math.log2(math.e)
NEG = -1e30
GRAIN = 32
BLOCK = 256
PART = 0.6
FRACTIONS = ((0.525, 0.675, 1.0), (0.45, 0.6375, 1.0))
F32 = jnp.float32
BF16 = jnp.bfloat16


def up(x, m):
    return (x + m - 1) // m * m


def dot_nt(a, b):
    return lax.dot_general(a, b, (((1,), (1,)), ((), ())), preferred_element_type=F32)


def dot_nn(a, b):
    return lax.dot_general(a, b, (((1,), (0,)), ((), ())), preferred_element_type=F32)


def dot_tn(a, b):
    return lax.dot_general(a, b, (((0,), (0,)), ((), ())), preferred_element_type=F32)


def query_blocks(rows):
    return [(q0, min(BLOCK, rows - q0)) for q0 in range(0, rows, BLOCK)]


def mask_of(q0, w, diagonal, low=None):
    k0, kn = (q0, w) if diagonal else (0, q0)
    key = k0 + lax.broadcasted_iota(jnp.int32, (kn, w), 0)
    query = q0 + lax.broadcasted_iota(jnp.int32, (1, w), 1)
    if low is None:
        return key <= query
    return (key >= low) & (key <= query) if diagonal else key >= low


def masked(x, q0, w, other, low=None):
    below = jnp.where(mask_of(q0, w, True, low), x[q0:], other)
    if not q0:
        return below
    above = x[:q0] if low is None else jnp.where(mask_of(q0, w, False, low), x[:q0], other)
    return jnp.concatenate([above, below], axis=0)


def staggered(blocks, front, back):
    held = None
    for block in blocks:
        fresh = front(*block)
        if held is not None:
            back(*held)
        held = (*block, fresh)
    back(*held)


def column(meta, s):
    return pl.ds(pl.multiple_of(meta[s] * HDIM, HDIM), HDIM)


def written_out(start, stop, copies, compute):
    def finish(s):
        for copy in copies(s):
            copy.wait()

    def step(s, c):
        @pl.when(s >= start + 2)
        def _():
            finish(s - 2)

        compute(s)
        for copy in copies(s):
            copy.start()
        return c

    lax.fori_loop(start, stop, step, 0)
    for back in (2, 1):

        @pl.when(stop - back >= start)
        def _(back=back):
            finish(stop - back)


def meta_kernel(heads, rows, caps, shift_ref, order_ref, out_ref, flag_ref):
    base = lax.axis_index("head") * heads
    for h in range(heads):
        flag_ref[h] = 0
    for i in range(HEADS // 2):
        loc = order_ref[i] - base

        @pl.when((loc >= 0) & (loc < heads))
        def _():
            flag_ref[loc] = 1

    count = flag_ref[0]
    for h in range(1, heads):
        count = count + flag_ref[h]
    yes, no = jnp.int32(0), count
    for h in range(heads):
        flag = flag_ref[h]
        out_ref[jnp.where(flag > 0, yes, no)] = h
        yes, no = yes + flag, no + 1 - flag
    off = shift_ref[0]
    late = jnp.where(2 * off > rows, 1, 0)
    far = (off + GRAIN - 1) // GRAIN * GRAIN
    near = rows - off // GRAIN * GRAIN
    slot = jnp.where(late > 0, near, far)
    early, tail = jnp.int32(1), jnp.int32(1 + len(caps[0]))
    for cap in caps[0][:-1]:
        early = early + jnp.where(count * slot > cap, 1, 0)
    for cap in caps[1][:-1]:
        tail = tail + jnp.where(count * slot > cap, 1, 0)
    pick = jnp.where(count > 0, jnp.where(late > 0, tail, early), 0)
    out_ref[heads] = count
    out_ref[heads + 1] = off
    out_ref[heads + 2] = slot
    out_ref[heads + 3] = pick


def pack_kernel(heads, rows, base, sizes, late, meta, a_ref, b_ref, one_ref, two_ref, sem, mid_ref):
    count, slot = meta[heads], meta[heads + 2]
    skip = rows - slot if late else 0
    split = one_ref.shape[0]

    def each(act):
        def step(s, c):
            column = pl.multiple_of(meta[s] * HDIM, HDIM)
            low = s * slot
            for ref, shift, mine in (
                (one_ref, low, low + slot <= split),
                (two_ref, low - split, low >= split),
                (mid_ref, 0, (low < split) & (low + slot > split)),
            ):

                def copy(at, size, i, ref=ref, shift=shift):
                    src = pl.multiple_of(skip + at, GRAIN)
                    dst = pl.multiple_of(shift + at, GRAIN)
                    for j, from_ref in enumerate((a_ref, b_ref)):
                        act(
                            pltpu.make_async_copy(
                                from_ref.at[pl.ds(src, size), pl.ds(column, HDIM)],
                                ref.at[pl.ds(dst, size), pl.ds(j * HDIM, HDIM)],
                                sem.at[s, j, i],
                            )
                        )

                @pl.when(mine)
                def _(copy=copy):
                    copy(0, base, 0)
                    at = jnp.int32(base)
                    for i, size in enumerate(sizes):
                        bit = ((slot - base) // size) % 2

                        @pl.when(bit == 1)
                        def _(at=at, size=size, i=i):
                            copy(at, size, i + 1)

                        at = at + bit * size

            return c

        lax.fori_loop(0, count, step, 0)

    each(lambda copy: copy.start())
    each(lambda copy: copy.wait())
    low = split // slot * slot
    cut = split - low

    @pl.when((low < count * slot) & (cut > 0))
    def _():
        def front(i, c):
            src = pl.multiple_of(i * GRAIN, GRAIN)
            dst = pl.multiple_of(low + i * GRAIN, GRAIN)
            one_ref[pl.ds(dst, GRAIN), :] = mid_ref[pl.ds(src, GRAIN), :]
            return c

        def rest(i, c):
            src = pl.multiple_of(cut + i * GRAIN, GRAIN)
            dst = pl.multiple_of(i * GRAIN, GRAIN)
            two_ref[pl.ds(dst, GRAIN), :] = mid_ref[pl.ds(src, GRAIN), :]
            return c

        lax.fori_loop(0, cut // GRAIN, front, 0)
        lax.fori_loop(0, (slot - cut) // GRAIN, rest, 0)


def stats_kernel(heads, rows, reach, meta, q_ref, k_ref, v_ref, d_ref, send_ref, own_ref):
    off = meta[heads + 1]

    def step(s, c):
        col = column(meta, s)

        def front(q0, w):
            kn = q0 + w
            sc = dot_nt(k_ref[:kn, col], q_ref[q0:kn, col]) * LOG2_SCALE
            return sc, dot_nt(v_ref[:kn, col], d_ref[q0:kn, col])

        def back(q0, w, held):
            sc, dp = held
            kn = q0 + w
            query = q0 + lax.broadcasted_iota(jnp.int32, (1, w), 1)
            sc = masked(sc, q0, w, NEG, jnp.where(query >= off, off, 0))
            top = jnp.max(sc, axis=0, keepdims=True)
            e = jnp.exp2(sc - top)
            total = jnp.sum(e, axis=0, keepdims=True)
            rd = jnp.sum(e * dp, axis=0, keepdims=True) / total
            lse = top + jnp.log2(total)
            own_ref[s, 0:1, q0:kn] = lse
            own_ref[s, 1:2, q0:kn] = rd
            if q0 < reach:
                send_ref[s, 0:1, q0:kn] = lse
                send_ref[s, 1:2, q0:kn] = rd

        staggered(query_blocks(rows), front, back)
        return c

    lax.fori_loop(0, meta[heads], step, 0)


def plain_kernel(
    heads, rows, meta, q_ref, k_ref, v_ref, d_ref, dq_ref, dk_ref, dv_ref,
    oq_ref, ok_ref, ov_ref, ak_ref, av_ref, sem,
):
    def copies(s):
        return [
            pltpu.make_async_copy(stage.at[s % 2], out.at[:, column(meta, s)], sem.at[s % 2, i])
            for i, (stage, out) in enumerate(((oq_ref, dq_ref), (ok_ref, dk_ref), (ov_ref, dv_ref)))
        ]

    def compute(s):
        col = column(meta, s)

        def front(q0, w):
            kn = q0 + w
            sc = dot_nt(k_ref[:kn, col], q_ref[q0:kn, col]) * LOG2_SCALE
            sc = masked(sc, q0, w, NEG)
            dp = dot_nt(v_ref[:kn, col], d_ref[q0:kn, col])
            top = jnp.max(sc, axis=0, keepdims=True)
            e = jnp.exp2(sc - top)
            inv = 1.0 / jnp.sum(e, axis=0, keepdims=True)
            rd = jnp.sum(e * dp, axis=0, keepdims=True) * inv
            p = e * inv
            return p.astype(BF16), (p * (dp - rd)).astype(BF16)

        def back(q0, w, held):
            accumulate(q0, w, held, col)

        def accumulate(q0, w, held, col):
            p, ds = held
            kn = q0 + w
            gv = dot_nn(p, d_ref[q0:kn, col])
            gk = dot_nn(ds, q_ref[q0:kn, col])
            oq_ref[s % 2, q0:kn, :] = (dot_tn(ds, k_ref[:kn, col]) * SCALE).astype(BF16)
            if q0:
                av_ref[:q0, :] += gv[:q0]
                ak_ref[:q0, :] += gk[:q0]
            av_ref[q0:kn, :] = gv[q0:]
            ak_ref[q0:kn, :] = gk[q0:]

        staggered(query_blocks(rows), front, back)
        ok_ref[s % 2] = (ak_ref[...] * SCALE).astype(BF16)
        ov_ref[s % 2] = av_ref[...].astype(BF16)

    written_out(meta[heads], heads, copies, compute)


def cross_kernel(heads, rows, first, half, reach, split, late, later, meta, *refs):
    refs = list(refs)
    a_ref, b_ref, one_ref = refs[:3]
    del refs[:3]
    two_ref = refs.pop(0) if later else None
    st_ref = refs.pop(0)
    passed = refs[: 3 if late else 4] if later else ()
    del refs[: len(passed) if later else 1]
    if late:
        back_ref, tot_ref, xq_ref, buf_ref, acc_ref, sum_ref = refs
        kept = ((tot_ref, 1), (xq_ref, 2))
    else:
        back_ref, tot_ref, gk_ref, gv_ref, buf_ref, acc_ref = refs
        kept = ((tot_ref, 1), (gk_ref, 2), (gv_ref, 3))
    count, off, slot = meta[heads], meta[heads + 1], meta[heads + 2]
    done = jnp.minimum(count, split // slot)
    low, high = (done, count) if later else (0, done)

    def move(dst_ref, src_ref, start, stop, shift):
        def step(i, c):
            dst = pl.multiple_of(start + i * GRAIN, GRAIN)
            src = pl.multiple_of(start - shift + i * GRAIN, GRAIN)
            dst_ref[pl.ds(dst, GRAIN), :] = src_ref[pl.ds(src, GRAIN), :]
            return c

        lax.fori_loop(0, (stop - start) // GRAIN, step, 0)

    @pl.when(low < high)
    def _():
        filled = high * slot
        if later:
            edge = jnp.minimum(filled, split)
            move(buf_ref, one_ref, low * slot, edge, 0)
            move(buf_ref, two_ref, edge, filled, split)
        else:
            move(buf_ref, one_ref, 0, filled, 0)
        tail = pl.multiple_of(filled, GRAIN)
        buf_ref[pl.ds(tail, BLOCK), :] = jnp.zeros((BLOCK, 2 * HDIM), BF16)

    def scores(s, lanes, inside, valid, kb, vb, qb, db):
        sc = jnp.where(valid, dot_nt(kb, qb) * LOG2_SCALE, NEG)
        dp = dot_nt(vb, db)
        top = jnp.max(sc, axis=0, keepdims=True)
        e = jnp.exp2(sc - top)
        total = jnp.sum(e, axis=0, keepdims=True)
        rd = jnp.sum(e * dp, axis=0, keepdims=True) / total
        lse = top + jnp.log2(total)
        lse1 = jnp.where(inside, st_ref[s, 0:1, lanes], 0.0)
        rd1 = jnp.where(inside, st_ref[s, 1:2, lanes], 0.0)
        most = jnp.maximum(lse, lse1)
        both = most + jnp.log2(jnp.exp2(lse - most) + jnp.exp2(lse1 - most))
        rd = jnp.exp2(lse - both) * rd + jnp.exp2(lse1 - both) * rd1
        tot_ref[s, 0:1, lanes] = both
        tot_ref[s, 1:2, lanes] = rd
        p = e * jnp.where(inside, jnp.exp2(top - both), 0.0)
        return p.astype(BF16), (p * (dp - rd)).astype(BF16)

    def keys_came(s, c):
        col = column(meta, s)
        mine = pl.ds(pl.multiple_of(s * slot, GRAIN), half)
        kb, vb = buf_ref[mine, :HDIM], buf_ref[mine, HDIM:]
        place = lax.broadcasted_iota(jnp.int32, (half, BLOCK), 0)
        valid = (place >= off - (rows - slot)) & (place < slot)

        def front(q0):
            lanes = slice(q0, q0 + BLOCK)
            inside = q0 + lax.broadcasted_iota(jnp.int32, (1, BLOCK), 1) < off
            return scores(s, lanes, inside, valid, kb, vb, a_ref[lanes, col], b_ref[lanes, col])

        def back(q0, held):
            p, ds = held
            lanes = slice(q0, q0 + BLOCK)
            gk, gv = dot_nn(ds, a_ref[lanes, col]), dot_nn(p, b_ref[lanes, col])
            if q0:
                gk, gv = sum_ref[0] + gk, sum_ref[1] + gv
            if q0 + BLOCK < reach:
                sum_ref[0], sum_ref[1] = gk, gv
            else:
                acc_ref[mine, :HDIM] = (gk * SCALE).astype(BF16)
                acc_ref[mine, HDIM:] = gv.astype(BF16)
            xq_ref[s, lanes, :] = dot_tn(ds, kb)

        staggered([(q0,) for q0 in range(0, reach, BLOCK)], front, back)
        return c

    def queries_came(s, c):
        col = column(meta, s)
        gk_ref[s] = jnp.zeros(gk_ref.shape[1:], F32)
        gv_ref[s] = jnp.zeros(gv_ref.shape[1:], F32)

        def block(j, c):
            q0 = pl.multiple_of(j * BLOCK, BLOCK)
            mine = pl.ds(pl.multiple_of(s * slot + q0, GRAIN), BLOCK)
            qb, db = buf_ref[mine, :HDIM], buf_ref[mine, HDIM:]
            kb = a_ref[first:, col]
            valid = first + lax.broadcasted_iota(jnp.int32, (rows - first, BLOCK), 0) >= off
            inside = q0 + lax.broadcasted_iota(jnp.int32, (1, BLOCK), 1) < off
            p, ds = scores(s, pl.ds(q0, BLOCK), inside, valid, kb, b_ref[first:, col], qb, db)
            gv_ref[s] += dot_nn(p, db)
            gk_ref[s] += dot_nn(ds, qb)
            acc_ref[mine, :] = (dot_tn(ds, kb) * SCALE).astype(BF16)
            return c

        lax.fori_loop(0, (off + BLOCK - 1) // BLOCK, block, 0)
        return c

    if later:

        def forward(s, c):
            for ref, i in kept:
                ref[s] = passed[i][s]
            return c

        lax.fori_loop(0, low, forward, 0)
    lax.fori_loop(low, high, keys_came if late else queries_came, 0)
    if later:
        move(back_ref, passed[0], 0, low * slot, 0)
    move(back_ref, acc_ref, low * slot, high * slot, 0)


def local_kernel(heads, rows, first, half, reach, late, meta, q_ref, k_ref, v_ref, d_ref, own_ref, tot_ref, *refs):
    refs = list(refs)
    if late:
        xq_ref = refs.pop(0)
    else:
        gk_ref, gv_ref = refs[:2]
        del refs[:2]
    del refs[:3]
    dq_ref, dk_ref, dv_ref = refs[:3]
    parts = refs[3 : 5 if late else 4]
    oq_ref, ok_ref, ov_ref, ak_ref, av_ref, sem = refs[5 if late else 4 :]
    off = meta[heads + 1]
    keys_out, query_out = (pl.ds(0, half), pl.ds(0, rows)) if late else (pl.ds(0, rows), pl.ds(half, rows - half))
    skip = 0 if late else half

    def copies(s):
        col = column(meta, s)
        return [
            pltpu.make_async_copy(stage.at[s % 2], out.at[span, col], sem.at[s % 2, i])
            for i, (stage, out, span) in enumerate(
                ((oq_ref, dq_ref, query_out), (ok_ref, dk_ref, keys_out), (ov_ref, dv_ref, keys_out))
            )
        ]

    def compute(s):
        col = column(meta, s)

        def front(q0, w):
            kn = q0 + w
            query = q0 + lax.broadcasted_iota(jnp.int32, (1, w), 1)
            lse, rd = own_ref[s, 0:1, q0:kn], own_ref[s, 1:2, q0:kn]
            if q0 < reach:
                lse = jnp.where(query < off, tot_ref[s, 0:1, q0:kn], lse)
                rd = jnp.where(query < off, tot_ref[s, 1:2, q0:kn], rd)
            sc = dot_nt(k_ref[:kn, col], q_ref[q0:kn, col]) * LOG2_SCALE
            p = masked(jnp.exp2(sc - lse), q0, w, 0.0, jnp.where(query >= off, off, 0))
            dp = dot_nt(v_ref[:kn, col], d_ref[q0:kn, col])
            return p.astype(BF16), (p * (dp - rd)).astype(BF16)

        def back(q0, w, held):
            p, ds = held
            kn = q0 + w
            gv = dot_nn(p, d_ref[q0:kn, col])
            gk = dot_nn(ds, q_ref[q0:kn, col])
            dq = dot_tn(ds, k_ref[:kn, col])
            if late and q0 < reach:
                dq = dq + xq_ref[s, q0:kn, :]
            dq = dq * SCALE
            if not late and q0 < half:
                parts[0][s, q0 : min(kn, half), :] = dq[: half - q0]
            at = max(q0, skip)
            if at < kn:
                oq_ref[s % 2, at - skip : kn - skip, :] = dq[at - q0 :].astype(BF16)
            if q0:
                av_ref[:q0, :] += gv[:q0]
                ak_ref[:q0, :] += gk[:q0]
            av_ref[q0:kn, :] = gv[q0:]
            ak_ref[q0:kn, :] = gk[q0:]

        staggered(query_blocks(rows), front, back)
        if late:
            ok_ref[s % 2] = (ak_ref[:half, :] * SCALE).astype(BF16)
            ov_ref[s % 2] = av_ref[:half, :].astype(BF16)
            parts[0][s] = ak_ref[half:, :] * SCALE
            parts[1][s] = av_ref[half:, :]
        else:
            ok_ref[s % 2, :first, :] = (ak_ref[:first, :] * SCALE).astype(BF16)
            ov_ref[s % 2, :first, :] = av_ref[:first, :].astype(BF16)
            ok_ref[s % 2, first:, :] = ((ak_ref[first:, :] + gk_ref[s]) * SCALE).astype(BF16)
            ov_ref[s % 2, first:, :] = (av_ref[first:, :] + gv_ref[s]).astype(BF16)

    written_out(0, meta[heads], copies, compute)


def add_kernel(heads, rows, half, late, meta, *refs):
    n = 2 if late else 1
    parts, got_ref, outs, stages, sem = refs[:n], refs[n], refs[2 * n + 1 : 3 * n + 1], refs[3 * n + 1 : 4 * n + 1], refs[-1]
    slot = meta[heads + 2]
    size = rows - half if late else half
    skip = size - slot if late else 0
    span = pl.ds(half if late else 0, size)

    def copies(s):
        col = column(meta, s)
        return [
            pltpu.make_async_copy(stage.at[s], out.at[span, col], sem.at[s, i])
            for i, (stage, out) in enumerate(zip(stages, outs))
        ]

    def send(s, c):
        def both(i, c):
            at = pl.ds(pl.multiple_of(skip + i * GRAIN, GRAIN), GRAIN)
            src = pl.ds(pl.multiple_of(s * slot + i * GRAIN, GRAIN), GRAIN)
            for j in range(n):
                there = got_ref[src, j * HDIM : (j + 1) * HDIM].astype(F32)
                stages[j][s, at, :] = (parts[j][s, at, :] + there).astype(BF16)
            return c

        def here(i, c):
            at = pl.ds(pl.multiple_of((0 if late else slot) + i * GRAIN, GRAIN), GRAIN)
            for j in range(n):
                stages[j][s, at, :] = parts[j][s, at, :].astype(BF16)
            return c

        lax.fori_loop(0, slot // GRAIN, both, 0)
        lax.fori_loop(0, (size - slot) // GRAIN, here, 0)
        for copy in copies(s):
            copy.start()
        return c

    def wait(s, c):
        for copy in copies(s):
            copy.wait()
        return c

    lax.fori_loop(0, meta[heads], send, 0)
    lax.fori_loop(0, meta[heads], wait, 0)


def cost(flops, moved):
    return pl.CostEstimate(flops=int(flops), bytes_accessed=int(moved), transcendentals=0)


def params(mebibytes):
    return pltpu.CompilerParams(vmem_limit_bytes=mebibytes * 2**20)


def shards(queries, keys, values, d_out, shift, head_order):
    rows, width = queries.shape
    heads = width // HDIM
    first, half = rows // 4, up(rows // 2, GRAIN)
    base = first // GRAIN * GRAIN
    reach = up(rows - first, BLOCK)
    most = heads * half
    caps = [[up(int(most * f), GRAIN) for f in group] for group in FRACTIONS]
    seq = lax.axis_size("seq")
    back = [(i, (i - 1) % seq) for i in range(seq)]
    ahead = [(i, (i + 1) % seq) for i in range(seq)]

    meta = pl.pallas_call(
        functools.partial(meta_kernel, heads, rows, caps),
        out_shape=jax.ShapeDtypeStruct((heads + 4,), jnp.int32),
        in_specs=[pl.BlockSpec(memory_space=pltpu.SMEM)] * 2,
        out_specs=pl.BlockSpec(memory_space=pltpu.SMEM),
        scratch_shapes=[pltpu.SMEM((heads,), jnp.int32)],
        name="meta",
    )(shift, head_order)

    whole = jax.ShapeDtypeStruct((rows, width), BF16)
    any_spec = pl.BlockSpec(memory_space=pl.ANY)
    vmem = pl.BlockSpec(memory_space=pltpu.VMEM)
    smem = pl.BlockSpec(memory_space=pltpu.SMEM)
    tile = rows * HDIM * 2
    work = 2 * rows * rows * HDIM

    def stages(*sizes):
        stage = [pltpu.VMEM((2, n, HDIM), BF16) for n in sizes]
        sums = [pltpu.VMEM((rows, HDIM), F32)] * 2
        return stage + sums + [pltpu.SemaphoreType.DMA((2, 3))]

    def call(kernel, in_specs, out_specs, out_shape, estimate, limit, scratch=(), aliases={}):
        return pl.pallas_call(
            kernel,
            out_shape=out_shape,
            in_specs=[smem] + in_specs,
            out_specs=out_specs,
            scratch_shapes=list(scratch),
            input_output_aliases=aliases,
            cost_estimate=estimate,
            compiler_params=params(limit),
        )

    def plain(meta, queries, keys, values, d_out):
        return call(
            functools.partial(plain_kernel, heads, rows),
            [vmem] * 4,
            [any_spec] * 3,
            [whole] * 3,
            cost(heads / 2 * 4 * work, heads / 2 * 7 * tile),
            16,
            stages(rows, rows, rows),
        )(meta, queries, keys, values, d_out)

    def rows_f32(n):
        return jax.ShapeDtypeStruct((heads, n, HDIM), F32)

    def pair(n):
        return jax.ShapeDtypeStruct((heads, 2, n), F32)

    def branch(cap, late):
        there, home = (ahead, back) if late else (back, ahead)
        wide = 2 * HDIM if late else HDIM
        split = up(int(cap * PART), GRAIN)

        def cross(later, meta, ours, *args):
            size = cap if later else split
            scratch = [pltpu.VMEM((size + half, 2 * HDIM), BF16), pltpu.VMEM((size + half, wide), BF16)]
            if late:
                scratch.append(pltpu.VMEM((2, half, HDIM), F32))
            return call(
                functools.partial(cross_kernel, heads, rows, first, half, reach, split, late, later),
                [vmem] * (2 + len(args)) if later else [vmem] * 4 + [any_spec],
                [vmem] * (3 if late else 4),
                [jax.ShapeDtypeStruct((size, wide), BF16), pair(reach)]
                + ([rows_f32(reach)] if late else [rows_f32(rows - first)] * 2),
                cost(heads / 4 * 5 * work, heads / 4 * 6 * tile),
                20,
                scratch,
            )(meta, *ours, *args)

        def steps(meta, queries, keys, values, d_out):
            inputs = (queries, keys, values, d_out)
            sizes, left = [], half - base
            while sum(sizes) < left:
                sizes.append(GRAIN * 2 ** len(sizes))
            one, two = call(
                functools.partial(pack_kernel, heads, rows, base, sizes, late),
                [any_spec] * 2,
                [vmem] * 2,
                [jax.ShapeDtypeStruct((n, 2 * HDIM), BF16) for n in (split, cap - split)],
                cost(0, 2 * cap * HDIM * 4),
                8,
                [
                    pltpu.SemaphoreType.DMA((heads, 2, 1 + len(sizes))),
                    pltpu.VMEM((half, 2 * HDIM), BF16),
                ],
            )(meta, *((keys, values) if late else (queries, d_out)))
            one_got = lax.ppermute(one, "seq", there)
            st_send, st_own = call(
                functools.partial(stats_kernel, heads, rows, reach),
                [vmem] * 4,
                [vmem, vmem],
                [pair(reach), pair(rows)],
                cost(heads / 2 * 2 * work, heads / 2 * 4 * tile),
                16,
            )(meta, *inputs)
            st = st_own
            if not late:
                st = lax.ppermute(st_send, "seq", there)
            two_got = lax.ppermute(two, "seq", there)
            grads = plain(meta, *inputs)
            ours = (queries, d_out) if late else (keys, values)
            begun = cross(False, meta, ours, one_got, st, grads[0])
            returned, tot, *side = cross(True, meta, ours, one_got, two_got, st, *begun)
            if not late:
                tot = lax.ppermute(tot, "seq", home)
            came = lax.ppermute(returned, "seq", home)
            mine = (1, 2) if late else (0,)
            n, at = len(mine), 7 + len(side)
            size = rows - half if late else half
            *grads, = call(
                functools.partial(local_kernel, heads, rows, first, half, reach, late),
                [vmem] * (6 + len(side)) + [any_spec] * 3,
                [any_spec] * 3 + [vmem] * n,
                [whole] * 3 + [rows_f32(size)] * n,
                cost(heads / 2 * 4 * work, heads / 2 * 9 * tile),
                24,
                stages(rows, half, half) if late else stages(rows - half, rows, rows),
                {at + i: i for i in range(3)},
            )(meta, *inputs, st_own, tot, *side, *grads)
            parts = grads[3:]
            added = call(
                functools.partial(add_kernel, heads, rows, half, late),
                [vmem] * (n + 1) + [any_spec] * n,
                [any_spec] * n,
                [whole] * n,
                cost(0, heads / 2 * 3 * tile),
                16,
                [pltpu.VMEM((heads, size, HDIM), BF16)] * n + [pltpu.SemaphoreType.DMA((heads, n))],
                {n + 2 + i: i for i in range(n)},
            )(meta, *parts, came, *[grads[i] for i in mine])
            for i, x in zip(mine, added):
                grads[i] = x
            return tuple(grads[:3])

        return steps

    branches = [lambda *args: tuple(plain(*args))]
    for late in (False, True):
        branches += [branch(cap, late) for cap in caps[late]]
    return lax.switch(meta[heads + 3], branches, meta, queries, keys, values, d_out)


def solution(mesh):
    spec = P(("rep", "seq"), "head")
    return jax.shard_map(
        shards,
        mesh=mesh,
        in_specs=(spec, spec, spec, spec, P("rep"), P()),
        out_specs=(spec, spec, spec),
        check_vma=False,
    )
```

```python
import functools
import math

import jax
import jax.numpy as jnp
from jax import lax
from jax.experimental import pallas as pl
from jax.experimental.pallas import tpu as pltpu
from jax.sharding import PartitionSpec as P


HEADS = 32
HDIM = 128
SCALE = HDIM ** (-0.5)
LOG2_SCALE = SCALE * math.log2(math.e)
NEG = -1e30
GRAIN = 32
BLOCK = 256
PART = 0.6
FRACTIONS = ((0.525, 0.675, 1.0), (0.45, 0.6375, 1.0))
F32 = jnp.float32
BF16 = jnp.bfloat16


def up(x, m):
    return (x + m - 1) // m * m


def dot_nt(a, b):
    return lax.dot_general(a, b, (((1,), (1,)), ((), ())), preferred_element_type=F32)


def dot_nn(a, b):
    return lax.dot_general(a, b, (((1,), (0,)), ((), ())), preferred_element_type=F32)


def dot_tn(a, b):
    return lax.dot_general(a, b, (((0,), (0,)), ((), ())), preferred_element_type=F32)


def query_blocks(rows):
    return [(q0, min(BLOCK, rows - q0)) for q0 in range(0, rows, BLOCK)]


def mask_of(q0, w, diagonal, low=None):
    k0, kn = (q0, w) if diagonal else (0, q0)
    key = k0 + lax.broadcasted_iota(jnp.int32, (kn, w), 0)
    query = q0 + lax.broadcasted_iota(jnp.int32, (1, w), 1)
    if low is None:
        return key <= query
    return (key >= low) & (key <= query) if diagonal else key >= low


def masked(x, q0, w, other, low=None):
    below = jnp.where(mask_of(q0, w, True, low), x[q0:], other)
    if not q0:
        return below
    above = x[:q0] if low is None else jnp.where(mask_of(q0, w, False, low), x[:q0], other)
    return jnp.concatenate([above, below], axis=0)


def staggered(blocks, front, back):
    held = None
    for block in blocks:
        fresh = front(*block)
        if held is not None:
            back(*held)
        held = (*block, fresh)
    back(*held)


def column(meta, s):
    return pl.ds(pl.multiple_of(meta[s] * HDIM, HDIM), HDIM)


def written_out(start, stop, copies, compute):
    def finish(s):
        for copy in copies(s):
            copy.wait()

    def step(s, c):
        @pl.when(s >= start + 2)
        def _():
            finish(s - 2)

        compute(s)
        for copy in copies(s):
            copy.start()
        return c

    lax.fori_loop(start, stop, step, 0)
    for back in (2, 1):

        @pl.when(stop - back >= start)
        def _(back=back):
            finish(stop - back)


def meta_kernel(heads, rows, caps, shift_ref, order_ref, out_ref, pick_ref, flag_ref):
    base = lax.axis_index("head") * heads
    for h in range(heads):
        flag_ref[h] = 0
    for i in range(HEADS // 2):
        loc = order_ref[i] - base

        @pl.when((loc >= 0) & (loc < heads))
        def _():
            flag_ref[loc] = 1

    count = flag_ref[0]
    for h in range(1, heads):
        count = count + flag_ref[h]
    yes, no = jnp.int32(0), count
    for h in range(heads):
        flag = flag_ref[h]
        out_ref[jnp.where(flag > 0, yes, no)] = h
        yes, no = yes + flag, no + 1 - flag
    off = shift_ref[0]
    late = jnp.where(2 * off > rows, 1, 0)
    far = (off + GRAIN - 1) // GRAIN * GRAIN
    near = rows - off // GRAIN * GRAIN
    slot = jnp.where(late > 0, near, far)
    early, tail = jnp.int32(1), jnp.int32(1 + len(caps[0]))
    for cap in caps[0][:-1]:
        early = early + jnp.where(count * slot > cap, 1, 0)
    for cap in caps[1][:-1]:
        tail = tail + jnp.where(count * slot > cap, 1, 0)
    pick = jnp.where(count > 0, jnp.where(late > 0, tail, early), 0)
    out_ref[heads] = count
    out_ref[heads + 1] = off
    out_ref[heads + 2] = slot
    pick_ref[0] = pick


def pack_kernel(heads, rows, base, sizes, late, meta, a_ref, b_ref, one_ref, two_ref, sem, mid_ref):
    count, slot = meta[heads], meta[heads + 2]
    skip = rows - slot if late else 0
    split = one_ref.shape[0]

    def each(act):
        def step(s, c):
            column = pl.multiple_of(meta[s] * HDIM, HDIM)
            low = s * slot
            for ref, shift, mine in (
                (one_ref, low, low + slot <= split),
                (two_ref, low - split, low >= split),
                (mid_ref, 0, (low < split) & (low + slot > split)),
            ):

                def copy(at, size, i, ref=ref, shift=shift):
                    src = pl.multiple_of(skip + at, GRAIN)
                    dst = pl.multiple_of(shift + at, GRAIN)
                    for j, from_ref in enumerate((a_ref, b_ref)):
                        act(
                            pltpu.make_async_copy(
                                from_ref.at[pl.ds(src, size), pl.ds(column, HDIM)],
                                ref.at[pl.ds(dst, size), pl.ds(j * HDIM, HDIM)],
                                sem.at[s, j, i],
                            )
                        )

                @pl.when(mine)
                def _(copy=copy):
                    copy(0, base, 0)
                    at = jnp.int32(base)
                    for i, size in enumerate(sizes):
                        bit = ((slot - base) // size) % 2

                        @pl.when(bit == 1)
                        def _(at=at, size=size, i=i):
                            copy(at, size, i + 1)

                        at = at + bit * size

            return c

        lax.fori_loop(0, count, step, 0)

    each(lambda copy: copy.start())
    each(lambda copy: copy.wait())
    low = split // slot * slot
    cut = split - low

    @pl.when((low < count * slot) & (cut > 0))
    def _():
        def front(i, c):
            src = pl.multiple_of(i * GRAIN, GRAIN)
            dst = pl.multiple_of(low + i * GRAIN, GRAIN)
            one_ref[pl.ds(dst, GRAIN), :] = mid_ref[pl.ds(src, GRAIN), :]
            return c

        def rest(i, c):
            src = pl.multiple_of(cut + i * GRAIN, GRAIN)
            dst = pl.multiple_of(i * GRAIN, GRAIN)
            two_ref[pl.ds(dst, GRAIN), :] = mid_ref[pl.ds(src, GRAIN), :]
            return c

        lax.fori_loop(0, cut // GRAIN, front, 0)
        lax.fori_loop(0, (slot - cut) // GRAIN, rest, 0)


def stats_kernel(heads, rows, reach, late, meta, q_ref, k_ref, v_ref, d_ref, send_ref, own_ref):
    def step(s, c):
        off = jnp.where(s < meta[heads], meta[heads + 1], 0)
        col = column(meta, s)

        def front(q0, w):
            kn = q0 + w
            sc = dot_nt(k_ref[:kn, col], q_ref[q0:kn, col]) * LOG2_SCALE
            return sc, dot_nt(v_ref[:kn, col], d_ref[q0:kn, col])

        def back(q0, w, held):
            sc, dp = held
            kn = q0 + w
            query = q0 + lax.broadcasted_iota(jnp.int32, (1, w), 1)
            sc = masked(sc, q0, w, NEG, jnp.where(query >= off, off, 0))
            top = jnp.max(sc, axis=0, keepdims=True)
            e = jnp.exp2(sc - top)
            total = jnp.sum(e, axis=0, keepdims=True)
            rd = jnp.sum(e * dp, axis=0, keepdims=True) / total
            lse = top + jnp.log2(total)
            own_ref[s, 0:1, q0:kn] = lse
            own_ref[s, 1:2, q0:kn] = rd
            if q0 < reach:
                send_ref[s, 0:1, q0:kn] = lse
                send_ref[s, 1:2, q0:kn] = rd

        staggered(query_blocks(rows), front, back)
        return c

    lax.fori_loop(0, heads if late else meta[heads], step, 0)


def plain_kernel(
    heads, rows, meta, q_ref, k_ref, v_ref, d_ref, dq_ref, dk_ref, dv_ref,
    oq_ref, ok_ref, ov_ref, ak_ref, av_ref, sem,
):
    def copies(s):
        return [
            pltpu.make_async_copy(stage.at[s % 2], out.at[:, column(meta, s)], sem.at[s % 2, i])
            for i, (stage, out) in enumerate(((oq_ref, dq_ref), (ok_ref, dk_ref), (ov_ref, dv_ref)))
        ]

    def compute(s):
        col = column(meta, s)

        def front(q0, w):
            kn = q0 + w
            sc = dot_nt(k_ref[:kn, col], q_ref[q0:kn, col]) * LOG2_SCALE
            sc = masked(sc, q0, w, NEG)
            dp = dot_nt(v_ref[:kn, col], d_ref[q0:kn, col])
            top = jnp.max(sc, axis=0, keepdims=True)
            e = jnp.exp2(sc - top)
            inv = 1.0 / jnp.sum(e, axis=0, keepdims=True)
            rd = jnp.sum(e * dp, axis=0, keepdims=True) * inv
            p = e * inv
            return p.astype(BF16), (p * (dp - rd)).astype(BF16)

        def back(q0, w, held):
            accumulate(q0, w, held, col)

        def accumulate(q0, w, held, col):
            p, ds = held
            kn = q0 + w
            gv = dot_nn(p, d_ref[q0:kn, col])
            gk = dot_nn(ds, q_ref[q0:kn, col])
            oq_ref[s % 2, q0:kn, :] = (dot_tn(ds, k_ref[:kn, col]) * SCALE).astype(BF16)
            if q0:
                av_ref[:q0, :] += gv[:q0]
                ak_ref[:q0, :] += gk[:q0]
            av_ref[q0:kn, :] = gv[q0:]
            ak_ref[q0:kn, :] = gk[q0:]

        staggered(query_blocks(rows), front, back)
        ok_ref[s % 2] = (ak_ref[...] * SCALE).astype(BF16)
        ov_ref[s % 2] = av_ref[...].astype(BF16)

    written_out(meta[heads], heads, copies, compute)


def cross_kernel(heads, rows, first, half, reach, split, late, later, meta, *refs):
    refs = list(refs)
    a_ref, b_ref, one_ref = refs[:3]
    del refs[:3]
    two_ref = refs.pop(0) if later else None
    st_ref = refs.pop(0)
    passed = refs[: 3 if late else 4] if later else ()
    del refs[: len(passed) if later else 0 if late else 1]
    if late:
        back_ref, tot_ref, xq_ref, buf_ref, acc_ref, sum_ref = refs
        kept = ((tot_ref, 1), (xq_ref, 2))
    else:
        back_ref, tot_ref, gk_ref, gv_ref, buf_ref, acc_ref = refs
        kept = ((tot_ref, 1), (gk_ref, 2), (gv_ref, 3))
    count, off, slot = meta[heads], meta[heads + 1], meta[heads + 2]
    wide = up(half, 128)
    done = jnp.minimum(count, split // slot)
    low, high = (done, count) if later else (0, done)

    def move(dst_ref, src_ref, start, stop, shift):
        def step(i, c):
            dst = pl.multiple_of(start + i * GRAIN, GRAIN)
            src = pl.multiple_of(start - shift + i * GRAIN, GRAIN)
            dst_ref[pl.ds(dst, GRAIN), :] = src_ref[pl.ds(src, GRAIN), :]
            return c

        lax.fori_loop(0, (stop - start) // GRAIN, step, 0)

    @pl.when(low < high)
    def _():
        filled = high * slot
        if later:
            edge = jnp.minimum(filled, split)
            move(buf_ref, one_ref, low * slot, edge, 0)
            move(buf_ref, two_ref, edge, filled, split)
        else:
            move(buf_ref, one_ref, 0, filled, 0)
        tail = pl.multiple_of(filled, GRAIN)
        buf_ref[pl.ds(tail, BLOCK), :] = jnp.zeros((BLOCK, 2 * HDIM), BF16)

    def scores(s, lanes, inside, valid, kb, vb, qb, db):
        sc = jnp.where(valid, dot_nt(kb, qb) * LOG2_SCALE, NEG)
        dp = dot_nt(vb, db)
        top = jnp.max(sc, axis=0, keepdims=True)
        e = jnp.exp2(sc - top)
        total = jnp.sum(e, axis=0, keepdims=True)
        rd = jnp.sum(e * dp, axis=0, keepdims=True) / total
        lse = top + jnp.log2(total)
        lse1 = jnp.where(inside, st_ref[s, 0:1, lanes], 0.0)
        rd1 = jnp.where(inside, st_ref[s, 1:2, lanes], 0.0)
        most = jnp.maximum(lse, lse1)
        both = most + jnp.log2(jnp.exp2(lse - most) + jnp.exp2(lse1 - most))
        rd = jnp.exp2(lse - both) * rd + jnp.exp2(lse1 - both) * rd1
        tot_ref[s, 0:1, lanes] = both
        tot_ref[s, 1:2, lanes] = rd
        p = e * jnp.where(inside, jnp.exp2(top - both), 0.0)
        return p.astype(BF16), (p * (dp - rd)).astype(BF16)

    def keys_came(s, c):
        col = column(meta, s)
        mine = pl.ds(pl.multiple_of(s * slot, GRAIN), half)
        kb, vb = buf_ref[mine, :HDIM], buf_ref[mine, HDIM:]
        place = lax.broadcasted_iota(jnp.int32, (half, BLOCK), 0)
        valid = (place >= off - (rows - slot)) & (place < slot)

        def front(q0):
            lanes = slice(q0, q0 + BLOCK)
            inside = q0 + lax.broadcasted_iota(jnp.int32, (1, BLOCK), 1) < off
            return scores(s, lanes, inside, valid, kb, vb, a_ref[lanes, col], b_ref[lanes, col])

        def back(q0, held):
            p, ds = held
            lanes = slice(q0, q0 + BLOCK)
            gk, gv = dot_nn(ds, a_ref[lanes, col]), dot_nn(p, b_ref[lanes, col])
            if q0:
                gk, gv = sum_ref[0] + gk, sum_ref[1] + gv
            if q0 + BLOCK < reach:
                sum_ref[0], sum_ref[1] = gk, gv
            else:
                acc_ref[mine, :HDIM] = (gk * SCALE).astype(BF16)
                acc_ref[mine, HDIM:] = gv.astype(BF16)
            xq_ref[s, lanes, :] = dot_tn(ds, kb)

        staggered([(q0,) for q0 in range(0, reach, BLOCK)], front, back)
        return c

    def queries_came(s, c):
        col = column(meta, s)
        for lanes, k0, fits in ((BLOCK, first, off <= BLOCK), (wide, BLOCK, off > BLOCK)):

            @pl.when(fits)
            def _(lanes=lanes, k0=k0):
                mine = pl.ds(pl.multiple_of(s * slot, GRAIN), lanes)
                qb, db = buf_ref[mine, :HDIM], buf_ref[mine, HDIM:]
                kb = a_ref[k0:, col]
                valid = k0 + lax.broadcasted_iota(jnp.int32, (rows - k0, lanes), 0) >= off
                inside = lax.broadcasted_iota(jnp.int32, (1, lanes), 1) < off
                p, ds = scores(s, slice(0, lanes), inside, valid, kb, b_ref[k0:, col], qb, db)
                gv_ref[s, k0 - first :, :] = dot_nn(p, db)
                gk_ref[s, k0 - first :, :] = dot_nn(ds, qb)
                if k0 > first:
                    gv_ref[s, : k0 - first, :] = jnp.zeros((k0 - first, HDIM), F32)
                    gk_ref[s, : k0 - first, :] = jnp.zeros((k0 - first, HDIM), F32)
                acc_ref[mine, :] = (dot_tn(ds, kb) * SCALE).astype(BF16)

        return c

    if later:

        def forward(s, c):
            for ref, i in kept:
                ref[s] = passed[i][s]
            return c

        lax.fori_loop(0, low, forward, 0)
    lax.fori_loop(low, high, keys_came if late else queries_came, 0)
    if later:
        move(back_ref, passed[0], 0, low * slot, 0)
    move(back_ref, acc_ref, low * slot, high * slot, 0)


def local_kernel(heads, rows, first, half, reach, late, meta, q_ref, k_ref, v_ref, d_ref, own_ref, tot_ref, *refs):
    refs = list(refs)
    if late:
        xq_ref = refs.pop(0)
    else:
        gk_ref, gv_ref = refs[:2]
        del refs[:5]
    dq_ref, dk_ref, dv_ref = refs[:3]
    parts = refs[3 : 5 if late else 4]
    oq_ref, ok_ref, ov_ref, ak_ref, av_ref, sem = refs[5 if late else 4 :]
    count = meta[heads]
    skip = 0 if late else half
    keys_out, query_out = pl.ds(0, rows), pl.ds(skip, rows - skip)

    def copies(s):
        col = column(meta, s)
        return [
            pltpu.make_async_copy(stage.at[s % 2], out.at[span, col], sem.at[s % 2, i])
            for i, (stage, out, span) in enumerate(
                ((oq_ref, dq_ref, query_out), (ok_ref, dk_ref, keys_out), (ov_ref, dv_ref, keys_out))
            )
        ]

    def compute(s):
        off = jnp.where(s < count, meta[heads + 1], 0)
        col = column(meta, s)

        def front(q0, w):
            kn = q0 + w
            query = q0 + lax.broadcasted_iota(jnp.int32, (1, w), 1)
            lse, rd = own_ref[s, 0:1, q0:kn], own_ref[s, 1:2, q0:kn]
            if q0 < reach:
                lse = jnp.where(query < off, tot_ref[s, 0:1, q0:kn], lse)
                rd = jnp.where(query < off, tot_ref[s, 1:2, q0:kn], rd)
            sc = dot_nt(k_ref[:kn, col], q_ref[q0:kn, col]) * LOG2_SCALE
            p = masked(jnp.exp2(sc - lse), q0, w, 0.0, jnp.where(query >= off, off, 0))
            dp = dot_nt(v_ref[:kn, col], d_ref[q0:kn, col])
            return p.astype(BF16), (p * (dp - rd)).astype(BF16)

        def back(q0, w, held):
            p, ds = held
            kn = q0 + w
            gv = dot_nn(p, d_ref[q0:kn, col])
            gk = dot_nn(ds, q_ref[q0:kn, col])
            dq = dot_tn(ds, k_ref[:kn, col])
            if late and q0 < reach:
                dq = dq + jnp.where(s < count, xq_ref[s, q0:kn, :], 0.0)
            dq = dq * SCALE
            if not late and q0 < half:
                parts[0][s, q0 : min(kn, half), :] = dq[: half - q0]
            at = max(q0, skip)
            if at < kn:
                oq_ref[s % 2, at - skip : kn - skip, :] = dq[at - q0 :].astype(BF16)
            if q0:
                av_ref[:q0, :] += gv[:q0]
                ak_ref[:q0, :] += gk[:q0]
            av_ref[q0:kn, :] = gv[q0:]
            ak_ref[q0:kn, :] = gk[q0:]

        staggered(query_blocks(rows), front, back)
        if late:
            ok_ref[s % 2] = (ak_ref[...] * SCALE).astype(BF16)
            ov_ref[s % 2] = av_ref[...].astype(BF16)
            parts[0][s] = ak_ref[half:, :] * SCALE
            parts[1][s] = av_ref[half:, :]
        else:
            ok_ref[s % 2, :first, :] = (ak_ref[:first, :] * SCALE).astype(BF16)
            ov_ref[s % 2, :first, :] = av_ref[:first, :].astype(BF16)
            ok_ref[s % 2, first:, :] = ((ak_ref[first:, :] + gk_ref[s]) * SCALE).astype(BF16)
            ov_ref[s % 2, first:, :] = (av_ref[first:, :] + gv_ref[s]).astype(BF16)

    written_out(0, heads if late else count, copies, compute)


def add_kernel(heads, rows, half, late, meta, *refs):
    n = 2 if late else 1
    parts, got_ref, outs, stages, sem = refs[:n], refs[n], refs[2 * n + 1 : 3 * n + 1], refs[3 * n + 1 : 4 * n + 1], refs[-1]
    slot = meta[heads + 2]
    size = rows - half if late else half
    skip = size - slot if late else 0
    span = pl.ds(half if late else 0, size)

    def copies(s):
        col = column(meta, s)
        return [
            pltpu.make_async_copy(stage.at[s], out.at[span, col], sem.at[s, i])
            for i, (stage, out) in enumerate(zip(stages, outs))
        ]

    def send(s, c):
        def both(i, c):
            at = pl.ds(pl.multiple_of(skip + i * GRAIN, GRAIN), GRAIN)
            src = pl.ds(pl.multiple_of(s * slot + i * GRAIN, GRAIN), GRAIN)
            for j in range(n):
                there = got_ref[src, j * HDIM : (j + 1) * HDIM].astype(F32)
                stages[j][s, at, :] = (parts[j][s, at, :] + there).astype(BF16)
            return c

        def here(i, c):
            at = pl.ds(pl.multiple_of((0 if late else slot) + i * GRAIN, GRAIN), GRAIN)
            for j in range(n):
                stages[j][s, at, :] = parts[j][s, at, :].astype(BF16)
            return c

        lax.fori_loop(0, slot // GRAIN, both, 0)
        lax.fori_loop(0, (size - slot) // GRAIN, here, 0)
        for copy in copies(s):
            copy.start()
        return c

    def wait(s, c):
        for copy in copies(s):
            copy.wait()
        return c

    lax.fori_loop(0, meta[heads], send, 0)
    lax.fori_loop(0, meta[heads], wait, 0)


def cost(flops, moved):
    return pl.CostEstimate(flops=int(flops), bytes_accessed=int(moved), transcendentals=0)


def params(mebibytes):
    return pltpu.CompilerParams(vmem_limit_bytes=mebibytes * 2**20)


def shards(queries, keys, values, d_out, shift, head_order):
    rows, width = queries.shape
    heads = width // HDIM
    first, half = rows // 4, up(rows // 2, GRAIN)
    base = first // GRAIN * GRAIN
    reach = up(rows - first, BLOCK)
    most = heads * half
    caps = [[up(int(most * f), GRAIN) for f in group] for group in FRACTIONS]
    seq = lax.axis_size("seq")
    back = [(i, (i - 1) % seq) for i in range(seq)]
    ahead = [(i, (i + 1) % seq) for i in range(seq)]

    meta, pick = pl.pallas_call(
        functools.partial(meta_kernel, heads, rows, caps),
        out_shape=[jax.ShapeDtypeStruct((heads + 3,), jnp.int32), jax.ShapeDtypeStruct((1,), jnp.int32)],
        in_specs=[pl.BlockSpec(memory_space=pltpu.SMEM)] * 2,
        out_specs=[pl.BlockSpec(memory_space=pltpu.SMEM)] * 2,
        scratch_shapes=[pltpu.SMEM((heads,), jnp.int32)],
        name="meta",
    )(shift, head_order)

    whole = jax.ShapeDtypeStruct((rows, width), BF16)
    any_spec = pl.BlockSpec(memory_space=pl.ANY)
    vmem = pl.BlockSpec(memory_space=pltpu.VMEM)
    smem = pl.BlockSpec(memory_space=pltpu.SMEM)
    tile = rows * HDIM * 2
    work = 2 * rows * rows * HDIM

    def stages(*sizes):
        stage = [pltpu.VMEM((2, n, HDIM), BF16) for n in sizes]
        sums = [pltpu.VMEM((rows, HDIM), F32)] * 2
        return stage + sums + [pltpu.SemaphoreType.DMA((2, 3))]

    def call(kernel, in_specs, out_specs, out_shape, estimate, limit, scratch=(), aliases={}):
        return pl.pallas_call(
            kernel,
            out_shape=out_shape,
            in_specs=[smem] + in_specs,
            out_specs=out_specs,
            scratch_shapes=list(scratch),
            input_output_aliases=aliases,
            cost_estimate=estimate,
            compiler_params=params(limit),
        )

    def plain(meta, queries, keys, values, d_out):
        return call(
            functools.partial(plain_kernel, heads, rows),
            [vmem] * 4,
            [any_spec] * 3,
            [whole] * 3,
            cost(heads / 2 * 4 * work, heads / 2 * 7 * tile),
            16,
            stages(rows, rows, rows),
        )(meta, queries, keys, values, d_out)

    def rows_f32(n):
        return jax.ShapeDtypeStruct((heads, n, HDIM), F32)

    def pair(n):
        return jax.ShapeDtypeStruct((heads, 2, n), F32)

    def branch(cap, late):
        there, home = (ahead, back) if late else (back, ahead)
        wide = 2 * HDIM if late else HDIM
        split = up(int(cap * PART), GRAIN)

        def cross(later, meta, ours, *args):
            size = cap if later else split
            scratch = [pltpu.VMEM((size + half, 2 * HDIM), BF16), pltpu.VMEM((size + half, wide), BF16)]
            if late:
                scratch.append(pltpu.VMEM((2, half, HDIM), F32))
            return call(
                functools.partial(cross_kernel, heads, rows, first, half, reach, split, late, later),
                [vmem] * 4 + [any_spec] * (not late) if not later else [vmem] * (2 + len(args)),
                [vmem] * (3 if late else 4),
                [jax.ShapeDtypeStruct((size, wide), BF16), pair(reach)]
                + ([rows_f32(reach)] if late else [rows_f32(rows - first)] * 2),
                cost(heads / 4 * 5 * work, heads / 4 * 6 * tile),
                20,
                scratch,
            )(meta, *ours, *args)

        def steps(meta, queries, keys, values, d_out):
            inputs = (queries, keys, values, d_out)
            sizes, left = [], half - base
            while sum(sizes) < left:
                sizes.append(GRAIN * 2 ** len(sizes))
            one, two = call(
                functools.partial(pack_kernel, heads, rows, base, sizes, late),
                [any_spec] * 2,
                [vmem] * 2,
                [jax.ShapeDtypeStruct((n, 2 * HDIM), BF16) for n in (split, cap - split)],
                cost(0, 2 * cap * HDIM * 4),
                8,
                [
                    pltpu.SemaphoreType.DMA((heads, 2, 1 + len(sizes))),
                    pltpu.VMEM((half, 2 * HDIM), BF16),
                ],
            )(meta, *((keys, values) if late else (queries, d_out)))
            one_got = lax.ppermute(one, "seq", there)
            st_send, st_own = call(
                functools.partial(stats_kernel, heads, rows, reach, late),
                [vmem] * 4,
                [vmem, vmem],
                [pair(reach), pair(rows)],
                cost(heads / 2 * 2 * work, heads / 2 * 4 * tile),
                16,
            )(meta, *inputs)
            st = st_own
            if not late:
                st = lax.ppermute(st_send, "seq", there)
            two_got = lax.ppermute(two, "seq", there)
            grads = () if late else plain(meta, *inputs)
            ours = (queries, d_out) if late else (keys, values)
            begun = cross(False, meta, ours, one_got, st, *grads[:1])
            returned, tot, *side = cross(True, meta, ours, one_got, two_got, st, *begun)
            if not late:
                tot = lax.ppermute(tot, "seq", home)
            came = lax.ppermute(returned, "seq", home)
            mine = (1, 2) if late else (0,)
            n, at = len(mine), 7 + len(side)
            size = rows - half if late else half
            *grads, = call(
                functools.partial(local_kernel, heads, rows, first, half, reach, late),
                [vmem] * (6 + len(side)) + [any_spec] * len(grads),
                [any_spec] * 3 + [vmem] * n,
                [whole] * 3 + [rows_f32(size)] * n,
                cost(heads / 2 * 4 * work, heads / 2 * 9 * tile),
                24,
                stages(rows if late else rows - half, rows, rows),
                {at + i: i for i in range(len(grads))},
            )(meta, *inputs, st_own, tot, *side, *grads)
            parts = grads[3:]
            added = call(
                functools.partial(add_kernel, heads, rows, half, late),
                [vmem] * (n + 1) + [any_spec] * n,
                [any_spec] * n,
                [whole] * n,
                cost(0, heads / 2 * 3 * tile),
                16,
                [pltpu.VMEM((heads, size, HDIM), BF16)] * n + [pltpu.SemaphoreType.DMA((heads, n))],
                {n + 2 + i: i for i in range(n)},
            )(meta, *parts, came, *[grads[i] for i in mine])
            for i, x in zip(mine, added):
                grads[i] = x
            return tuple(grads[:3])

        return steps

    branches = [lambda *args: tuple(plain(*args))]
    for late in (False, True):
        branches += [branch(cap, late) for cap in caps[late]]
    return lax.switch(pick.reshape(()), branches, meta, queries, keys, values, d_out)


def solution(mesh):
    spec = P(("rep", "seq"), "head")
    return jax.shard_map(
        shards,
        mesh=mesh,
        in_specs=(spec, spec, spec, spec, P("rep"), P()),
        out_specs=(spec, spec, spec),
        check_vma=False,
    )
```
